256 devices in a mesh: vox: 64 (over y, x, z_lo), sen: 4 (over z_hi, core).
Axes of the slice: x: 4, y: 4, z: 8 (z_hi: 2, z_lo: 4; z = z_hi * 4 + z_lo), core: 2. Of those that a mesh axis runs over, the one named last changes fastest.
Arguments:
- image: float32 [64, 2, 512], P('vox'), may hold values from -6 to 6
- weights: bfloat16 [64, 4, 5, 1024, 1024], P('vox', 'sen'), may hold values from -0.0625 to 0.0625
- block_ids: int32 [64, 4, 5], P('vox', 'sen'), may hold values from 0 to 15
- offsets: int32 [64, 4, 5], P('vox', 'sen'), may hold values from 0 to 1984
- counts: int32 [64, 4], P('vox', 'sen'), may hold values from 1 to 5, as said below
- measured: bfloat16 [4, 256, 2048], P('sen', 'vox'), may hold values from -6 to 6
Outputs:
- image_next: float32 [64, 2, 512], P('vox')
- residual: float32 [4, 256, 2048], P('sen', 'vox')
The draws below stay inside these ranges and needn't reach their ends.
Inputs may be any that keep to these rules, and one draw needn't show every extreme that they name: `counts`: some slab and group has all 5 slots live in every draw.
All inputs are finite; a program needn't handle non-finite values.
Results may differ from the reference program's by a relative error of at most 0.0025.
Values may be sent and summed in bfloat16 or wider, within the bound.
No kernel may reach another device: no remote copies, remote signals or barrier semaphores. Data moves between devices by JAX's collectives and lax.ppermute only.
A program may use at most 64 MiB of HBM per device.

```python
import jax
import jax.numpy as jnp
from jax import lax

SAMPLES = 2048
SB = 16
WIN = 64
K_MAX = 5
ZS = 1
PY = 2
PX = 512
SLABS = 64
GROUPS = 4
GSENS = 256
BLOCKS = 16
NZ = 64


def draw_counts(key, part):
    first_key, second_key = jax.random.split(jax.random.fold_in(key, 17))
    drawn_counts = jax.random.randint(first_key, (SLABS, GROUPS), 1, K_MAX + 1)
    chosen = jax.random.randint(second_key, (), 0, SLABS * GROUPS)
    flat_index = jnp.arange(SLABS * GROUPS).reshape(SLABS, GROUPS)
    return jnp.where(flat_index == chosen, K_MAX, drawn_counts).astype(jnp.int32)


def touch_ends(drawn, key, least, largest):
    shape = drawn.shape
    spot = [jax.random.randint(jax.random.fold_in(key, axis), (), 0, shape[axis]) for axis in range(len(shape))]
    drawn = drawn.at[tuple(spot)].set(least)
    longest = shape.index(max(shape))
    spot[longest] = (spot[longest] + 1) % shape[longest]
    return drawn.at[tuple(spot)].set(largest)


def steps_of(rng, extent, cuts, low, high):
    gain, own = 1.0, jax.random.fold_in(rng, 6)
    for dim, blocks in cuts:
        draws = jnp.exp(jax.random.uniform(jax.random.fold_in(own, dim), (blocks,), jnp.float32, low / len(cuts), high / len(cuts)))
        gain = gain * jnp.repeat(draws, extent[dim] // blocks).reshape([-1 if axis == dim else 1 for axis in range(len(extent))])
    return gain


def normal_values(rng, shape, width, limit, cuts=(), held_as=jnp.bfloat16):
    loudness = steps_of(rng, shape, cuts, -0.22, 0.18) if cuts else 1.0
    array = jax.random.normal(rng, shape, jnp.float32) * width * loudness
    return jnp.minimum(jnp.maximum(array, -limit), limit).astype(held_as)


def setup_inputs(seed: int = 0) -> dict:
    arg_keys = jax.random.split(jax.random.key(seed), 7)
    return {
        "image": normal_values(arg_keys[0], (NZ, PY, PX), 1.0, 6.0, ((0, 64),), jnp.float32),
        "weights": normal_values(arg_keys[1], (SLABS, GROUPS, K_MAX, ZS * PY * PX, SB * WIN), (8 * SB * WIN) ** -0.5, 0.0625, ((0, 64), (1, 4))),
        "block_ids": touch_ends(jax.random.randint(arg_keys[2], (SLABS, GROUPS, K_MAX), 0, BLOCKS), jax.random.fold_in(arg_keys[2], 1), 0, BLOCKS - 1).astype(jnp.int32),
        "offsets": touch_ends(jax.random.randint(arg_keys[3], (SLABS, GROUPS, K_MAX), 0, SAMPLES - WIN + 1), jax.random.fold_in(arg_keys[3], 1), 0, SAMPLES - WIN).astype(jnp.int32),
        "counts": draw_counts(jax.random.fold_in(arg_keys[6], 71), 0),
        "measured": normal_values(arg_keys[5], (GROUPS, GSENS, SAMPLES), 1.0, 6.0, ((0, 4), (1, 64))),
    }


TAPS = ((-2, 1.0 / 12.0), (-1, -8.0 / 12.0), (1, 8.0 / 12.0), (2, -1.0 / 12.0))
STEP_SIZE = 0.25
TV_WEIGHT = 0.3
TV_EPS = 0.01

def derivative(signal):
    length_t = signal.shape[-1]
    padded = jnp.pad(signal, [(0, 0)] * (signal.ndim - 1) + [(2, 2)])
    summed = jnp.zeros_like(signal)
    for shift_by, coefficient in TAPS:
        summed = summed + coefficient * padded[..., 2 + shift_by:2 + shift_by + length_t]
    return summed

def forward_step(volume, axis_dim):
    length_a = volume.shape[axis_dim]
    ahead = jnp.concatenate([lax.slice_in_dim(volume, 1, length_a, axis=axis_dim), lax.slice_in_dim(volume, length_a - 1, length_a, axis=axis_dim)], axis=axis_dim)
    return ahead - volume

def backward_shift(field, axis_dim):
    length_a = field.shape[axis_dim]
    zero_row = jnp.zeros_like(lax.slice_in_dim(field, 0, 1, axis=axis_dim))
    return jnp.concatenate([zero_row, lax.slice_in_dim(field, 0, length_a - 1, axis=axis_dim)], axis=axis_dim)

def tv_gradient(volume):
    step_z = forward_step(volume, 0)
    step_y = forward_step(volume, 1)
    step_x = forward_step(volume, 2)
    magnitude = jnp.sqrt(step_z * step_z + step_y * step_y + step_x * step_x + TV_EPS)
    result = jnp.zeros_like(volume)
    for axis_dim, step_a in ((0, step_z), (1, step_y), (2, step_x)):
        unit_a = step_a / magnitude
        result = result + backward_shift(unit_a, axis_dim) - unit_a
    return result

def reference(image, weights, block_ids, offsets, counts, measured):
    voxels = image.astype(jnp.bfloat16).astype(jnp.float32).reshape(SLABS, ZS * PY * PX)
    slot_grid = jnp.arange(K_MAX, dtype=jnp.int32)

    def add_slab(signals, inputs):
        slab_voxels, slab_blocks, slab_ids, slab_starts, slab_counts = inputs
        pieces = jnp.einsum('v,gkvc->gkc', slab_voxels, slab_blocks.astype(jnp.float32))

        def place(flat_index, acc):
            group_index = (flat_index // K_MAX).astype(jnp.int32)
            slot_index = (flat_index % K_MAX).astype(jnp.int32)
            live_flag = (slot_index < slab_counts[group_index]).astype(jnp.float32)
            piece = pieces[group_index, slot_index].reshape(1, SB, WIN) * live_flag
            corner = (group_index, (slab_ids[group_index, slot_index] * SB).astype(jnp.int32), slab_starts[group_index, slot_index].astype(jnp.int32))
            current = lax.dynamic_slice(acc, corner, (1, SB, WIN))
            return lax.dynamic_update_slice(acc, current + piece, corner)
        signals = lax.fori_loop(0, GROUPS * K_MAX, place, signals)
        return (signals, None)
    zero_signals = jnp.zeros((GROUPS, GSENS, SAMPLES), jnp.float32)
    signals, _ = lax.scan(add_slab, zero_signals, (voxels, weights, block_ids, offsets, counts))
    residual = derivative(signals) - measured.astype(jnp.float32)
    adjoint = lax.optimization_barrier((-derivative(residual)).astype(jnp.bfloat16)).astype(jnp.float32)
    group_grid = jnp.broadcast_to(jnp.arange(GROUPS, dtype=jnp.int32)[:, None], (GROUPS, K_MAX))

    def cut_window(group_index, block_index, start):
        corner = (group_index, (block_index * SB).astype(jnp.int32), start.astype(jnp.int32))
        return lax.dynamic_slice(adjoint, corner, (1, SB, WIN)).reshape(SB * WIN)

    def back_slab(carry, inputs):
        slab_blocks, slab_ids, slab_starts, slab_counts = inputs
        windows = jax.vmap(jax.vmap(cut_window))(group_grid, slab_ids, slab_starts)
        live = (slot_grid[None, :] < slab_counts[:, None]).astype(jnp.float32)
        windows = windows * live[:, :, None]
        grad_slab = jnp.einsum('gkc,gkvc->v', windows, slab_blocks.astype(jnp.float32))
        return (carry, grad_slab)
    _, backprojected = lax.scan(back_slab, jnp.zeros((), jnp.float32), (weights, block_ids, offsets, counts))
    backprojected = backprojected.reshape(NZ, PY, PX)
    image_next = image - STEP_SIZE * (backprojected + TV_WEIGHT * tv_gradient(image))
    return (image_next, residual)
```

```python
import functools

import jax
import jax.numpy as jnp
from jax import lax
from jax.experimental import pallas as pl
from jax.experimental.pallas import tpu as pltpu
from jax.sharding import Mesh
from jax.sharding import PartitionSpec as P

SB = 16
WIN = 64
K_MAX = 5
VOXELS = 1024
CELLS = SB * WIN
LANES = 128
ROWS = 16
OWNERS = 64
CHUNKS = 2
STEP_SIZE = 0.25
TV_WEIGHT = 0.3
TV_EPS = 0.01
NOWHERE = 255.0
MIB = 1 << 20

VOX = ("y", "x", "z_lo")
SEN = ("z_hi", "core")


def lane_iota(shape):
    return lax.broadcasted_iota(jnp.int32, shape, len(shape) - 1)


def forward_kernel(ids, starts, counts, image, weights, measured, sent, spread, held, tiles, sems):
    depth = VOXELS // CHUNKS
    copies = {}
    for k in range(K_MAX):
        for c in range(CHUNKS):
            span = pl.ds(c * depth, depth)
            copies[k, c] = pltpu.make_async_copy(
                weights.at[0, 0, k, span], held.at[k, span], sems.at[k * CHUNKS + c]
            )
            copies[k, c].start()

    own = measured[0].astype(jnp.float32)
    for r in range(4):
        for h in range(16):
            spread[r * 16 + h : r * 16 + h + 1, :] = own[r : r + 1, h * LANES : (h + 1) * LANES]

    voxels = jnp.concatenate([image[0, 0:1, :], image[0, 1:2, :]], axis=1).astype(jnp.bfloat16)
    lane = lane_iota((8, LANES))
    row16 = lax.broadcasted_iota(jnp.int32, (ROWS, LANES), 0)
    lane16 = lane_iota((ROWS, LANES))
    base = jnp.full((ROWS, LANES), NOWHERE, jnp.float32)
    code_tile = jnp.full((ROWS, LANES), NOWHERE, jnp.float32)
    block_tile = jnp.full((ROWS, LANES), -1, jnp.int32)
    live = counts[0, 0]
    for k in range(K_MAX):
        start = starts[0, 0, k]
        coarse = start // WIN
        low = start - coarse * WIN
        code = (coarse & 1) * 16 + (coarse >> 1)
        block = jnp.where(k < live, ids[0, 0, k], -1)
        here = row16 == 10 + k
        base = jnp.where(here & (lane16 >= WIN), low.astype(jnp.float32), base)
        code_tile = jnp.where(here & (lane16 < WIN), code.astype(jnp.float32), code_tile)
        block_tile = jnp.where(here & (lane16 < WIN), block, block_tile)

    for k in range(K_MAX):
        piece = jnp.zeros((1, CELLS), jnp.float32)
        for c in range(CHUNKS):
            copies[k, c].wait()
            piece = piece + jnp.dot(
                voxels[:, c * depth : (c + 1) * depth],
                held[k, c * depth : (c + 1) * depth, :],
                preferred_element_type=jnp.float32,
            )
        tile = jnp.concatenate([piece[:, i * LANES : (i + 1) * LANES] for i in range(8)], axis=0)
        low = lax.rem(starts[0, 0, k], WIN)
        tile = jnp.where(
            (lane & (WIN - 1)) >= low, pltpu.roll(tile, low, 1), pltpu.roll(tile, low + WIN, 1)
        )
        for q in range(4):
            tiles[q, 2 * k : 2 * k + 2, :] = tile[2 * q : 2 * q + 2, :]

    for q in range(4):
        full = jnp.where(row16 < 10, tiles[q], base)
        for b in range(16):
            sent[4 * b + q] = jnp.where(block_tile == b, code_tile, full).astype(jnp.bfloat16)


def derivative(x):
    row = lax.broadcasted_iota(jnp.int32, x.shape, 0) & 15
    lane = lane_iota(x.shape)

    def ahead(t):
        rolled = pltpu.roll(x, LANES - t, 1)
        after = jnp.where(row == 15, 0.0, pltpu.roll(rolled, x.shape[0] - 1, 0))
        return jnp.where(lane >= LANES - t, after, rolled)

    def behind(t):
        rolled = pltpu.roll(x, t, 1)
        before = jnp.where(row == 0, 0.0, pltpu.roll(rolled, 1, 0))
        return jnp.where(lane < t, before, rolled)

    return ((behind(2) - ahead(2)) + 8.0 * (ahead(1) - behind(1))) * (1.0 / 12.0)


def owner_kernel(got, spread, sent, residual, wide):
    wide[...] = got[...].astype(jnp.float32).reshape(OWNERS * ROWS, LANES)
    lane = lane_iota((OWNERS, LANES))
    low_half = lane < WIN
    within = (lane & (WIN - 1)).astype(jnp.float32)
    slot = jnp.where(low_half, lane & 31, 0).astype(jnp.float32)
    places, strips, later = [], [], []
    for k in range(K_MAX):
        info = wide[pl.ds(10 + k, OWNERS, stride=ROWS), :]
        turned = pltpu.roll(info, WIN, 1)
        code = jnp.where(low_half, info, turned)
        low = jnp.where(low_half, turned, info)
        following = jnp.where(code >= 16.0, code - 15.0, code + 16.0)
        wanted = jnp.where(lane < 32, code, following)
        places.append(jnp.where(low_half & (wanted == slot), 1.0, 0.0))
        first = within >= low
        later.append(first)
        parts = []
        for u in range(2):
            strip = wide[pl.ds(2 * k + u, OWNERS, stride=ROWS), :]
            parts.append((jnp.where(first, strip, 0.0), jnp.where(first, 0.0, strip)))
        strips.append(
            jnp.concatenate([parts[0][0], parts[1][0], parts[0][1], parts[1][1]], axis=1)
        )
    place = jnp.concatenate(places, axis=0).astype(jnp.bfloat16)
    strip = jnp.concatenate(strips, axis=0).astype(jnp.bfloat16)
    both = lax.dot_general(
        place, strip, (((0,), (0,)), ((), ())), preferred_element_type=jnp.float32
    )
    summed = both[0:32, 0:256] + both[32:64, 256:512]
    lane16 = lane_iota((16, LANES)) < WIN
    rows = []
    for u in range(2):
        even = summed[0:16, u * LANES : (u + 1) * LANES]
        odd = summed[16:32, u * LANES : (u + 1) * LANES]
        rows.append(jnp.where(lane16, even, pltpu.roll(odd, WIN, 1)))
        rows.append(jnp.where(lane16, pltpu.roll(even, WIN, 1), odd))
    signals = jnp.concatenate(rows, axis=0)
    resid = derivative(signals) - spread[...]
    adjoint = -derivative(resid)
    packed = []
    for u in range(2):
        a = adjoint[32 * u : 32 * u + 16]
        b = adjoint[32 * u + 16 : 32 * u + 32]
        packed.append(
            (
                jnp.where(lane16, a, pltpu.roll(b, WIN, 1)),
                jnp.where(lane16, pltpu.roll(a, WIN, 1), b),
            )
        )
    table = jnp.concatenate(
        [jnp.concatenate([packed[0][p], packed[1][p]], axis=1) for p in range(2)], axis=0
    )
    zero = jnp.zeros_like(table)
    table = jnp.concatenate(
        [
            jnp.concatenate([table, zero], axis=1),
            jnp.concatenate([zero, table], axis=1),
            jnp.zeros((64, 512), jnp.float32),
        ],
        axis=0,
    ).astype(jnp.bfloat16)
    cut = jnp.dot(place, table, preferred_element_type=jnp.float32)
    for k in range(K_MAX):
        mine = cut[k * OWNERS : (k + 1) * OWNERS]
        for u in range(2):
            window = jnp.where(
                later[k],
                mine[:, u * LANES : (u + 1) * LANES],
                mine[:, 256 + u * LANES : 256 + (u + 1) * LANES],
            )
            wide[pl.ds(2 * k + u, OWNERS, stride=ROWS), :] = window
    sent[...] = wide[...].reshape(OWNERS, ROWS, LANES).astype(jnp.bfloat16)
    for r in range(4):
        for h in range(16):
            residual[0, r : r + 1, h * LANES : (h + 1) * LANES] = resid[
                r * 16 + h : r * 16 + h + 1, :
            ]


def total_variation(image, before, after, is_first, is_last):
    lane = lane_iota((2, 512))
    row = lax.broadcasted_iota(jnp.int32, (2, 512), 0)

    def units(here, ahead, no_step):
        step_z = jnp.where(no_step, 0.0, ahead - here)
        step_y = jnp.where(row == 1, 0.0, pltpu.roll(here, 1, 0) - here)
        step_x = jnp.where(lane == 511, 0.0, pltpu.roll(here, 511, 1) - here)
        magnitude = jnp.sqrt(step_z * step_z + step_y * step_y + step_x * step_x + TV_EPS)
        return step_z / magnitude, step_y / magnitude, step_x / magnitude

    unit_z, unit_y, unit_x = units(image, after, is_last)
    below_z, _, _ = units(before, image, is_first)
    result = below_z - unit_z
    result = result + (jnp.where(row == 0, 0.0, pltpu.roll(unit_y, 1, 0)) - unit_y)
    return result + (jnp.where(lane == 0, 0.0, pltpu.roll(unit_x, 1, 1)) - unit_x)


def backward_kernel(
    ids, starts, counts, got, weights, image, before, after, grad, base, held, wins, sems
):
    depth = VOXELS // CHUNKS
    copies = {}
    for k in range(K_MAX):
        for c in range(CHUNKS):
            span = pl.ds(c * depth, depth)
            copies[k, c] = pltpu.make_async_copy(
                weights.at[0, 0, k, span], held.at[k, span], sems.at[k * CHUNKS + c]
            )
            copies[k, c].start()
    vox = lax.axis_index(VOX)
    here = image[0]
    tv = total_variation(here, before[0], after[0], vox == 0, vox == OWNERS - 1)
    base[0] = here - (STEP_SIZE * TV_WEIGHT) * tv

    live = counts[0, 0]
    lane = lane_iota((8, LANES))
    vectors = []
    for k in range(K_MAX):
        block = ids[0, 0, k]
        for q in range(4):
            strip = got[4 * block + q].astype(jnp.float32)
            wins[2 * q : 2 * q + 2, :] = strip[2 * k : 2 * k + 2, :]
        low = lax.rem(starts[0, 0, k], WIN)
        tile = wins[...]
        tile = jnp.where(
            (lane & (WIN - 1)) < WIN - low,
            pltpu.roll(tile, lax.rem(LANES - low, LANES), 1),
            pltpu.roll(tile, WIN - low, 1),
        )
        tile = jnp.where(k < live, tile, 0.0)
        vectors.append(
            jnp.concatenate([tile[i : i + 1, :] for i in range(8)], axis=1).astype(jnp.bfloat16)
        )
    for c in range(CHUNKS):
        total = jnp.zeros((1, depth), jnp.float32)
        for k in range(K_MAX):
            copies[k, c].wait()
            total = total + lax.dot_general(
                vectors[k],
                held[k, c * depth : (c + 1) * depth, :],
                (((1,), (1,)), ((), ())),
                preferred_element_type=jnp.float32,
            )
        grad[0, c : c + 1, :] = total


def smem():
    return pl.BlockSpec(memory_space=pltpu.SMEM)


def vmem():
    return pl.BlockSpec(memory_space=pltpu.VMEM)


def anywhere():
    return pl.BlockSpec(memory_space=pl.ANY)


def held_scratch():
    return pltpu.VMEM((K_MAX, VOXELS, CELLS), jnp.bfloat16)


def on_device(image, weights, block_ids, offsets, counts, measured):
    before = lax.ppermute(image, VOX, [(i, i + 1) for i in range(OWNERS - 1)])
    after = lax.ppermute(image, VOX, [(i + 1, i) for i in range(OWNERS - 1)])
    sent, spread = pl.pallas_call(
        forward_kernel,
        out_shape=(
            jax.ShapeDtypeStruct((OWNERS, ROWS, LANES), jnp.bfloat16),
            jax.ShapeDtypeStruct((64, LANES), jnp.float32),
        ),
        in_specs=[smem(), smem(), smem(), vmem(), anywhere(), vmem()],
        out_specs=(vmem(), vmem()),
        scratch_shapes=[
            held_scratch(),
            pltpu.VMEM((4, ROWS, LANES), jnp.float32),
            pltpu.SemaphoreType.DMA((K_MAX * CHUNKS,)),
        ],
        compiler_params=pltpu.CompilerParams(vmem_limit_bytes=40 * MIB),
        name="forward",
    )(block_ids, offsets, counts, image, weights, measured)
    got = lax.all_to_all(sent, VOX, 0, 0, tiled=True)
    sent, residual = pl.pallas_call(
        owner_kernel,
        out_shape=(
            jax.ShapeDtypeStruct((OWNERS, ROWS, LANES), jnp.bfloat16),
            jax.ShapeDtypeStruct((1, 4, 2048), jnp.float32),
        ),
        in_specs=[vmem(), vmem()],
        out_specs=(vmem(), vmem()),
        scratch_shapes=[pltpu.VMEM((OWNERS * ROWS, LANES), jnp.float32)],
        compiler_params=pltpu.CompilerParams(vmem_limit_bytes=40 * MIB),
        name="owner",
    )(got, spread)
    got = lax.all_to_all(sent, VOX, 0, 0, tiled=True)
    grad, base = pl.pallas_call(
        backward_kernel,
        out_shape=(
            jax.ShapeDtypeStruct((1, 2, 512), jnp.float32),
            jax.ShapeDtypeStruct((1, 2, 512), jnp.float32),
        ),
        in_specs=[smem(), smem(), smem(), vmem(), anywhere(), vmem(), vmem(), vmem()],
        out_specs=(vmem(), vmem()),
        scratch_shapes=[
            held_scratch(),
            pltpu.VMEM((8, LANES), jnp.float32),
            pltpu.SemaphoreType.DMA((K_MAX * CHUNKS,)),
        ],
        compiler_params=pltpu.CompilerParams(vmem_limit_bytes=40 * MIB),
        name="backward",
    )(block_ids, offsets, counts, got, weights, image, before, after)
    grad = grad + lax.ppermute(grad, "core", [(0, 1), (1, 0)])
    grad = grad + lax.ppermute(grad, "z_hi", [(0, 1), (1, 0)])
    return (base - STEP_SIZE * grad, residual)


def solution(mesh):
    fine = Mesh(mesh.devices.reshape(4, 4, 4, 2, 2), VOX + SEN)
    placed = (
        P(VOX, None, None),
        P(VOX, SEN, None, None, None),
        P(VOX, SEN, None),
        P(VOX, SEN, None),
        P(VOX, SEN),
        P(SEN, VOX, None),
    )
    return jax.shard_map(
        on_device,
        mesh=fine,
        in_specs=placed,
        out_specs=(P(VOX, None, None), P(SEN, VOX, None)),
        check_vma=False,
    )
```

```python
import functools

import jax
import jax.numpy as jnp
from jax import lax
from jax.experimental import pallas as pl
from jax.experimental.pallas import tpu as pltpu
from jax.sharding import Mesh
from jax.sharding import PartitionSpec as P

SB = 16
WIN = 64
K_MAX = 5
VOXELS = 1024
CELLS = SB * WIN
LANES = 128
ROWS = 16
OWNERS = 64
CHUNKS = 2
STEP_SIZE = 0.25
TV_WEIGHT = 0.3
TV_EPS = 0.01
NOWHERE = 255.0
MIB = 1 << 20

VOX = ("y", "x", "z_lo")
SEN = ("z_hi", "core")


def lane_iota(shape):
    return lax.broadcasted_iota(jnp.int32, shape, len(shape) - 1)


def as_tile(image):
    rows = [image[0, y : y + 1, t * LANES : (t + 1) * LANES] for y in range(2) for t in range(4)]
    return jnp.concatenate(rows, axis=0)


def split_three(x):
    parts = []
    for _ in range(3):
        part = x.astype(jnp.bfloat16).astype(jnp.float32)
        parts.append(part)
        x = x - part
    return parts


def forward_kernel(
    ids_hbm,
    starts_hbm,
    counts,
    image_hbm,
    weights,
    measured_hbm,
    sent,
    spread,
    held,
    ids,
    starts,
    image,
    measured,
    tiles,
    halo,
    small_sems,
    sems,
):
    small = []
    for i, (src, dst) in enumerate(
        (
            (image_hbm, image),
            (ids_hbm, ids),
            (starts_hbm, starts),
            (measured_hbm, measured),
        )
    ):
        small.append(pltpu.make_async_copy(src, dst, small_sems.at[i]))
        small[-1].start()
    depth = VOXELS // CHUNKS
    copies = {}
    for k in range(K_MAX):
        for c in range(CHUNKS):
            span = pl.ds(c * depth, depth)
            copies[k, c] = pltpu.make_async_copy(
                weights.at[0, 0, k, span], held.at[k, span], sems.at[k * CHUNKS + c]
            )
            copies[k, c].start()
    for copy in small:
        copy.wait()

    own = measured[0].astype(jnp.float32)
    for r in range(4):
        for h in range(16):
            spread[r * 16 + h : r * 16 + h + 1, :] = own[r : r + 1, h * LANES : (h + 1) * LANES]

    plane = as_tile(image)
    turned = jnp.concatenate(split_three(plane) + [jnp.zeros((104, LANES), jnp.float32)], axis=0).T
    halo[...] = turned[0:64] + pltpu.roll(turned[64:128], 24, 1)

    voxels = jnp.concatenate([image[0, 0:1, :], image[0, 1:2, :]], axis=1).astype(jnp.bfloat16)
    lane = lane_iota((8, LANES))
    row = lax.broadcasted_iota(jnp.int32, (8, LANES), 0)
    base = jnp.full((8, LANES), NOWHERE, jnp.float32)
    code_tile = jnp.full((8, LANES), NOWHERE, jnp.float32)
    block_tile = jnp.full((8, LANES), -1, jnp.int32)
    live = counts[0, 0]
    for k in range(K_MAX):
        start = starts[0, 0, k]
        coarse = start // WIN
        low = start - coarse * WIN
        code = (coarse & 1) * 16 + (coarse >> 1)
        block = jnp.where(k < live, ids[0, 0, k], -1)
        here = row == 2 + k
        base = jnp.where(here & (lane >= WIN), low.astype(jnp.float32), base)
        code_tile = jnp.where(here & (lane < WIN), code.astype(jnp.float32), code_tile)
        block_tile = jnp.where(here & (lane < WIN), block, block_tile)

    for k in range(K_MAX):
        piece = jnp.zeros((1, CELLS), jnp.float32)
        for c in range(CHUNKS):
            copies[k, c].wait()
            piece = piece + jnp.dot(
                voxels[:, c * depth : (c + 1) * depth],
                held[k, c * depth : (c + 1) * depth, :],
                preferred_element_type=jnp.float32,
            )
        tile = jnp.concatenate([piece[:, i * LANES : (i + 1) * LANES] for i in range(8)], axis=0)
        low = lax.rem(starts[0, 0, k], WIN)
        tile = jnp.where(
            (lane & (WIN - 1)) >= low, pltpu.roll(tile, low, 1), pltpu.roll(tile, low + WIN, 1)
        )
        for q in range(4):
            tiles[q, 2 * k : 2 * k + 2, :] = tile[2 * q : 2 * q + 2, :]
        if k == 3:
            for q in range(4):
                data = tiles[q, 0:8, :].astype(jnp.bfloat16)
                for b in range(16):
                    sent[4 * b + q, 0:8, :] = data

    for q in range(4):
        full = jnp.where(row < 2, tiles[q, 8:16, :], base)
        for b in range(16):
            own_halo = jnp.broadcast_to(halo[4 * b + q : 4 * b + q + 1, :], (8, LANES))
            marked = jnp.where(block_tile == b, code_tile, full)
            sent[4 * b + q, 8:16, :] = jnp.where(row == 7, own_halo, marked).astype(jnp.bfloat16)


def derivative(x):
    row = lax.broadcasted_iota(jnp.int32, x.shape, 0) & 15
    lane = lane_iota(x.shape)

    def ahead(t):
        rolled = pltpu.roll(x, LANES - t, 1)
        after = jnp.where(row == 15, 0.0, pltpu.roll(rolled, x.shape[0] - 1, 0))
        return jnp.where(lane >= LANES - t, after, rolled)

    def behind(t):
        rolled = pltpu.roll(x, t, 1)
        before = jnp.where(row == 0, 0.0, pltpu.roll(rolled, 1, 0))
        return jnp.where(lane < t, before, rolled)

    return ((behind(2) - ahead(2)) + 8.0 * (ahead(1) - behind(1))) * (1.0 / 12.0)


def owner_kernel(got, spread, sent, residual, wide):
    wide[...] = got[...].astype(jnp.float32).reshape(OWNERS * ROWS, LANES)
    lane = lane_iota((OWNERS, LANES))
    low_half = lane < WIN
    within = (lane & (WIN - 1)).astype(jnp.float32)
    slot = jnp.where(low_half, lane & 31, 0).astype(jnp.float32)
    places, strips, later = [], [], []
    for k in range(K_MAX):
        info = wide[pl.ds(10 + k, OWNERS, stride=ROWS), :]
        turned = pltpu.roll(info, WIN, 1)
        code = jnp.where(low_half, info, turned)
        low = jnp.where(low_half, turned, info)
        following = jnp.where(code >= 16.0, code - 15.0, code + 16.0)
        wanted = jnp.where(lane < 32, code, following)
        places.append(jnp.where(low_half & (wanted == slot), 1.0, 0.0))
        first = within >= low
        later.append(first)
        parts = []
        for u in range(2):
            strip = wide[pl.ds(2 * k + u, OWNERS, stride=ROWS), :]
            parts.append((jnp.where(first, strip, 0.0), jnp.where(first, 0.0, strip)))
        strips.append(
            jnp.concatenate([parts[0][0], parts[1][0], parts[0][1], parts[1][1]], axis=1)
        )
    place = jnp.concatenate(places, axis=0).astype(jnp.bfloat16)
    strip = jnp.concatenate(strips, axis=0).astype(jnp.bfloat16)
    both = lax.dot_general(
        place, strip, (((0,), (0,)), ((), ())), preferred_element_type=jnp.float32
    )
    summed = both[0:32, 0:256] + both[32:64, 256:512]
    lane16 = lane_iota((16, LANES)) < WIN
    rows = []
    for u in range(2):
        even = summed[0:16, u * LANES : (u + 1) * LANES]
        odd = summed[16:32, u * LANES : (u + 1) * LANES]
        rows.append(jnp.where(lane16, even, pltpu.roll(odd, WIN, 1)))
        rows.append(jnp.where(lane16, pltpu.roll(even, WIN, 1), odd))
    signals = jnp.concatenate(rows, axis=0)
    resid = derivative(signals) - spread[...]
    adjoint = -derivative(resid)
    packed = []
    for u in range(2):
        a = adjoint[32 * u : 32 * u + 16]
        b = adjoint[32 * u + 16 : 32 * u + 32]
        packed.append(
            (
                jnp.where(lane16, a, pltpu.roll(b, WIN, 1)),
                jnp.where(lane16, pltpu.roll(a, WIN, 1), b),
            )
        )
    table = jnp.concatenate(
        [jnp.concatenate([packed[0][p], packed[1][p]], axis=1) for p in range(2)], axis=0
    )
    zero = jnp.zeros_like(table)
    table = jnp.concatenate(
        [
            jnp.concatenate([table, zero], axis=1),
            jnp.concatenate([zero, table], axis=1),
            jnp.zeros((64, 512), jnp.float32),
        ],
        axis=0,
    ).astype(jnp.bfloat16)
    cut = jnp.dot(place, table, preferred_element_type=jnp.float32)
    for k in range(K_MAX):
        mine = cut[k * OWNERS : (k + 1) * OWNERS]
        for u in range(2):
            window = jnp.where(
                later[k],
                mine[:, u * LANES : (u + 1) * LANES],
                mine[:, 256 + u * LANES : 256 + (u + 1) * LANES],
            )
            wide[pl.ds(2 * k + u, OWNERS, stride=ROWS), :] = window
    shard = wide[pl.ds(15, OWNERS, stride=ROWS), :]
    wide[pl.ds(10, OWNERS, stride=ROWS), :] = jnp.where(
        low_half,
        pltpu.roll(shard, 1, 0),
        pltpu.roll(pltpu.roll(shard, OWNERS - 1, 0), WIN, 1),
    )
    sent[...] = wide[...].reshape(OWNERS, ROWS, LANES).astype(jnp.bfloat16)
    for r in range(4):
        for h in range(16):
            residual[0, r : r + 1, h * LANES : (h + 1) * LANES] = resid[
                r * 16 + h : r * 16 + h + 1, :
            ]


def total_variation(image, before, after, is_first, is_last):
    lane = lane_iota((8, LANES))
    row = lax.broadcasted_iota(jnp.int32, (8, LANES), 0)
    last_x = (lane == LANES - 1) & ((row & 3) == 3)
    first_x = (lane == 0) & ((row & 3) == 0)

    def units(here, ahead, no_step):
        step_z = jnp.where(no_step, 0.0, ahead - here)
        step_y = jnp.where(row >= 4, 0.0, pltpu.roll(here, 4, 0) - here)
        moved = pltpu.roll(here, LANES - 1, 1)
        moved = jnp.where(lane == LANES - 1, pltpu.roll(moved, 7, 0), moved)
        step_x = jnp.where(last_x, 0.0, moved - here)
        magnitude = jnp.sqrt(step_z * step_z + step_y * step_y + step_x * step_x + TV_EPS)
        return step_z / magnitude, step_y / magnitude, step_x / magnitude

    unit_z, unit_y, unit_x = units(image, after, is_last)
    below_z, _, _ = units(before, image, is_first)
    result = below_z - unit_z
    result = result + (jnp.where(row < 4, 0.0, pltpu.roll(unit_y, 4, 0)) - unit_y)
    moved = pltpu.roll(unit_x, 1, 1)
    moved = jnp.where(lane == 0, pltpu.roll(moved, 1, 0), moved)
    return result + (jnp.where(first_x, 0.0, moved) - unit_x)


def smooth_kernel(got, image, base, wide):
    vox = lax.axis_index(VOX)
    wide[...] = got[:, 8:16, :].astype(jnp.float32).reshape(OWNERS * 8, LANES)
    shard = wide[pl.ds(2, OWNERS, stride=8), :]
    whole = shard + (pltpu.roll(shard, LANES - 8, 1) + pltpu.roll(shard, LANES - 16, 1))
    turned = jnp.concatenate([whole, pltpu.roll(whole, LANES - 24, 1)], axis=0).T
    here = as_tile(image)
    tv = total_variation(here, turned[0:8], turned[64:72], vox == 0, vox == OWNERS - 1)
    out = here - (STEP_SIZE * TV_WEIGHT) * tv
    for y in range(2):
        for t in range(4):
            base[0, y : y + 1, t * LANES : (t + 1) * LANES] = out[y * 4 + t : y * 4 + t + 1]


def backward_kernel(ids, starts, counts, got, held, grad, wins):
    depth = VOXELS // 2
    live = counts[0, 0]
    lane = lane_iota((8, LANES))
    vectors = []
    for k in range(K_MAX):
        block = ids[0, 0, k]
        for q in range(4):
            strip = got[4 * block + q].astype(jnp.float32)
            wins[2 * q : 2 * q + 2, :] = strip[2 * k : 2 * k + 2, :]
        low = lax.rem(starts[0, 0, k], WIN)
        tile = wins[...]
        tile = jnp.where(
            (lane & (WIN - 1)) < WIN - low,
            pltpu.roll(tile, lax.rem(LANES - low, LANES), 1),
            pltpu.roll(tile, WIN - low, 1),
        )
        tile = jnp.where(k < live, tile, 0.0)
        vectors.append(
            jnp.concatenate([tile[i : i + 1, :] for i in range(8)], axis=1).astype(jnp.bfloat16)
        )
    for c in range(2):
        total = jnp.zeros((1, depth), jnp.float32)
        for k in range(K_MAX):
            total = total + lax.dot_general(
                vectors[k],
                held[k, c * depth : (c + 1) * depth, :],
                (((1,), (1,)), ((), ())),
                preferred_element_type=jnp.float32,
            )
        grad[0, c : c + 1, :] = total


def smem():
    return pl.BlockSpec(memory_space=pltpu.SMEM)


def vmem():
    return pl.BlockSpec(memory_space=pltpu.VMEM)


def hbm():
    return pl.BlockSpec(memory_space=pltpu.HBM)


def in_hbm(array):
    return pltpu.with_memory_space_constraint(array, pltpu.HBM)


def on_device(image, weights, block_ids, offsets, counts, measured):
    sent, spread, held = pl.pallas_call(
        forward_kernel,
        out_shape=(
            jax.ShapeDtypeStruct((OWNERS, ROWS, LANES), jnp.bfloat16),
            jax.ShapeDtypeStruct((64, LANES), jnp.float32),
            jax.ShapeDtypeStruct((K_MAX, VOXELS, CELLS), jnp.bfloat16),
        ),
        in_specs=[hbm(), hbm(), smem(), hbm(), hbm(), hbm()],
        out_specs=(vmem(), vmem(), vmem()),
        scratch_shapes=[
            pltpu.SMEM((1, 1, K_MAX), jnp.int32),
            pltpu.SMEM((1, 1, K_MAX), jnp.int32),
            pltpu.VMEM((1, 2, 512), jnp.float32),
            pltpu.VMEM((1, 4, 2048), jnp.bfloat16),
            pltpu.VMEM((4, ROWS, LANES), jnp.float32),
            pltpu.VMEM((OWNERS, LANES), jnp.float32),
            pltpu.SemaphoreType.DMA((4,)),
            pltpu.SemaphoreType.DMA((K_MAX * CHUNKS,)),
        ],
        compiler_params=pltpu.CompilerParams(vmem_limit_bytes=20 * MIB),
        name="forward",
    )(
        in_hbm(block_ids),
        in_hbm(offsets),
        counts,
        in_hbm(image),
        in_hbm(weights),
        in_hbm(measured),
    )
    got = lax.all_to_all(sent, VOX, 0, 0, tiled=True)
    sent, residual = pl.pallas_call(
        owner_kernel,
        out_shape=(
            jax.ShapeDtypeStruct((OWNERS, ROWS, LANES), jnp.bfloat16),
            jax.ShapeDtypeStruct((1, 4, 2048), jnp.float32),
        ),
        in_specs=[vmem(), vmem()],
        out_specs=(vmem(), vmem()),
        scratch_shapes=[pltpu.VMEM((OWNERS * ROWS, LANES), jnp.float32)],
        compiler_params=pltpu.CompilerParams(vmem_limit_bytes=8 * MIB),
        name="owner",
    )(got, spread)
    got = lax.all_to_all(sent, VOX, 0, 0, tiled=True)
    grad = pl.pallas_call(
        backward_kernel,
        out_shape=jax.ShapeDtypeStruct((1, 2, 512), jnp.float32),
        in_specs=[smem(), smem(), smem(), vmem(), vmem()],
        out_specs=vmem(),
        scratch_shapes=[pltpu.VMEM((8, LANES), jnp.float32)],
        compiler_params=pltpu.CompilerParams(vmem_limit_bytes=20 * MIB),
        name="backward",
    )(block_ids, offsets, counts, got, held)
    grad = grad + lax.ppermute(grad, "core", [(0, 1), (1, 0)])
    other = lax.ppermute(grad, "z_hi", [(0, 1), (1, 0)])
    base = pl.pallas_call(
        smooth_kernel,
        out_shape=jax.ShapeDtypeStruct((1, 2, 512), jnp.float32),
        in_specs=[vmem(), vmem()],
        out_specs=vmem(),
        scratch_shapes=[pltpu.VMEM((OWNERS * 8, LANES), jnp.float32)],
        compiler_params=pltpu.CompilerParams(vmem_limit_bytes=8 * MIB),
        cost_estimate=pl.CostEstimate(flops=100000, bytes_accessed=1 << 19, transcendentals=4096),
        name="smooth",
    )(got, image)
    return (base - STEP_SIZE * (grad + other), residual)


def solution(mesh):
    fine = Mesh(mesh.devices.reshape(4, 4, 4, 2, 2), VOX + SEN)
    placed = (
        P(VOX, None, None),
        P(VOX, SEN, None, None, None),
        P(VOX, SEN, None),
        P(VOX, SEN, None),
        P(VOX, SEN),
        P(SEN, VOX, None),
    )
    return jax.shard_map(
        on_device,
        mesh=fine,
        in_specs=placed,
        out_specs=(P(VOX, None, None), P(SEN, VOX, None)),
        check_vma=False,
    )
```

```python
import functools

import jax
import jax.numpy as jnp
from jax import lax
from jax.experimental import pallas as pl
from jax.experimental.pallas import tpu as pltpu
from jax.sharding import Mesh
from jax.sharding import PartitionSpec as P

SB = 16
WIN = 64
K_MAX = 5
VOXELS = 1024
CELLS = SB * WIN
LANES = 128
ROWS = 16
OWNERS = 64
ON_MATRIX = 2
IN_FLIGHT = 3
STEP_SIZE = 0.25
TV_WEIGHT = 0.3
TV_EPS = 0.01
NOWHERE = 255.0
MIB = 1 << 20

VOX = ("y", "x", "z_lo")
SEN = ("z_hi", "core")


def lane_iota(shape):
    return lax.broadcasted_iota(jnp.int32, shape, len(shape) - 1)


def as_tile(image):
    rows = [image[0, y : y + 1, t * LANES : (t + 1) * LANES] for y in range(2) for t in range(4)]
    return jnp.concatenate(rows, axis=0)


def split_three(x):
    parts = []
    for _ in range(3):
        part = x.astype(jnp.bfloat16).astype(jnp.float32)
        parts.append(part)
        x = x - part
    return parts


def forward_kernel(
    ids_hbm,
    starts_hbm,
    counts,
    image_hbm,
    weights,
    measured_hbm,
    sent,
    spread,
    held,
    ids,
    starts,
    image,
    measured,
    tiles,
    halo,
    small_sems,
    sems,
):
    small = []
    for i, (src, dst) in enumerate(
        (
            (image_hbm, image),
            (ids_hbm, ids),
            (starts_hbm, starts),
            (measured_hbm, measured),
        )
    ):
        small.append(pltpu.make_async_copy(src, dst, small_sems.at[i]))
        small[-1].start()
    copies = [
        pltpu.make_async_copy(weights.at[0, 0, k], held.at[k], sems.at[k]) for k in range(K_MAX)
    ]
    for copy in copies[:IN_FLIGHT]:
        copy.start()
    for copy in small:
        copy.wait()

    own = measured[0].astype(jnp.float32)
    for r in range(4):
        for h in range(16):
            spread[r * 16 + h : r * 16 + h + 1, :] = own[r : r + 1, h * LANES : (h + 1) * LANES]

    plane = as_tile(image)
    turned = jnp.concatenate(split_three(plane) + [jnp.zeros((104, LANES), jnp.float32)], axis=0).T
    halo[...] = turned[0:64] + pltpu.roll(turned[64:128], 24, 1)

    voxels = jnp.concatenate([image[0, 0:1, :], image[0, 1:2, :]], axis=1).astype(jnp.bfloat16)
    lane = lane_iota((8, LANES))
    row = lax.broadcasted_iota(jnp.int32, (8, LANES), 0)
    base = jnp.full((8, LANES), NOWHERE, jnp.float32)
    code_tile = jnp.full((8, LANES), NOWHERE, jnp.float32)
    block_tile = jnp.full((8, LANES), -1, jnp.int32)
    live = counts[0, 0]
    for k in range(K_MAX):
        start = starts[0, 0, k]
        coarse = start // WIN
        low = start - coarse * WIN
        code = (coarse & 1) * 16 + (coarse >> 1)
        block = jnp.where(k < live, ids[0, 0, k], -1)
        here = row == 2 + k
        base = jnp.where(here & (lane >= WIN), low.astype(jnp.float32), base)
        code_tile = jnp.where(here & (lane < WIN), code.astype(jnp.float32), code_tile)
        block_tile = jnp.where(here & (lane < WIN), block, block_tile)

    for d in range(OWNERS):
        own_halo = jnp.broadcast_to(halo[d : d + 1, :], (8, LANES))
        marked = jnp.where(block_tile == d // 4, code_tile, base)
        sent[d, 8:16, :] = jnp.where(row == 7, own_halo, marked).astype(jnp.bfloat16)

    for k in range(K_MAX):
        copies[k].wait()
        if k + IN_FLIGHT < K_MAX:
            copies[k + IN_FLIGHT].start()
        piece = jnp.dot(voxels, held[k], preferred_element_type=jnp.float32)
        tile = jnp.concatenate([piece[:, i * LANES : (i + 1) * LANES] for i in range(8)], axis=0)
        low = lax.rem(starts[0, 0, k], WIN)
        tile = jnp.where(
            (lane & (WIN - 1)) >= low, pltpu.roll(tile, low, 1), pltpu.roll(tile, low + WIN, 1)
        )
        for q in range(4):
            tiles[q, 2 * k : 2 * k + 2, :] = tile[2 * q : 2 * q + 2, :]
        if k == 3:
            for q in range(4):
                data = tiles[q, 0:8, :].astype(jnp.bfloat16)
                for b in range(16):
                    sent[4 * b + q, 0:8, :] = data

    last = [tiles[q, 8:10, :].astype(jnp.bfloat16) for q in range(4)]
    for q in range(4):
        for b in range(16):
            sent[4 * b + q, 8:10, :] = last[q]


def derivative(x):
    row = lax.broadcasted_iota(jnp.int32, x.shape, 0) & 15
    lane = lane_iota(x.shape)

    def ahead(t):
        rolled = pltpu.roll(x, LANES - t, 1)
        after = jnp.where(row == 15, 0.0, pltpu.roll(rolled, x.shape[0] - 1, 0))
        return jnp.where(lane >= LANES - t, after, rolled)

    def behind(t):
        rolled = pltpu.roll(x, t, 1)
        before = jnp.where(row == 0, 0.0, pltpu.roll(rolled, 1, 0))
        return jnp.where(lane < t, before, rolled)

    return ((behind(2) - ahead(2)) + 8.0 * (ahead(1) - behind(1))) * (1.0 / 12.0)


def owner_kernel(got, spread, sent, residual, wide):
    wide[...] = got[...].astype(jnp.float32).reshape(OWNERS * ROWS, LANES)
    lane = lane_iota((OWNERS, LANES))
    low_half = lane < WIN
    within = (lane & (WIN - 1)).astype(jnp.float32)
    slot = jnp.where(low_half, lane & 31, 0).astype(jnp.float32)
    places, strips, later = [], [], []
    for k in range(K_MAX):
        info = wide[pl.ds(10 + k, OWNERS, stride=ROWS), :]
        turned = pltpu.roll(info, WIN, 1)
        code = jnp.where(low_half, info, turned)
        low = jnp.where(low_half, turned, info)
        following = jnp.where(code >= 16.0, code - 15.0, code + 16.0)
        wanted = jnp.where(lane < 32, code, following)
        places.append(jnp.where(low_half & (wanted == slot), 1.0, 0.0))
        first = within >= low
        later.append(first)
        parts = []
        for u in range(2):
            strip = wide[pl.ds(2 * k + u, OWNERS, stride=ROWS), :]
            parts.append((jnp.where(first, strip, 0.0), jnp.where(first, 0.0, strip)))
        strips.append(
            jnp.concatenate([parts[0][0], parts[1][0], parts[0][1], parts[1][1]], axis=1)
        )
    place = jnp.concatenate(places, axis=0).astype(jnp.bfloat16)
    strip = jnp.concatenate(strips, axis=0).astype(jnp.bfloat16)
    both = lax.dot_general(
        place, strip, (((0,), (0,)), ((), ())), preferred_element_type=jnp.float32
    )
    summed = both[0:32, 0:256] + both[32:64, 256:512]
    lane16 = lane_iota((16, LANES)) < WIN
    rows = []
    for u in range(2):
        even = summed[0:16, u * LANES : (u + 1) * LANES]
        odd = summed[16:32, u * LANES : (u + 1) * LANES]
        rows.append(jnp.where(lane16, even, pltpu.roll(odd, WIN, 1)))
        rows.append(jnp.where(lane16, pltpu.roll(even, WIN, 1), odd))
    signals = jnp.concatenate(rows, axis=0)
    resid = derivative(signals) - spread[...]
    adjoint = -derivative(resid)
    packed = []
    for u in range(2):
        a = adjoint[32 * u : 32 * u + 16]
        b = adjoint[32 * u + 16 : 32 * u + 32]
        packed.append(
            (
                jnp.where(lane16, a, pltpu.roll(b, WIN, 1)),
                jnp.where(lane16, pltpu.roll(a, WIN, 1), b),
            )
        )
    table = jnp.concatenate(
        [jnp.concatenate([packed[0][p], packed[1][p]], axis=1) for p in range(2)], axis=0
    )
    zero = jnp.zeros_like(table)
    table = jnp.concatenate(
        [
            jnp.concatenate([table, zero], axis=1),
            jnp.concatenate([zero, table], axis=1),
            jnp.zeros((64, 512), jnp.float32),
        ],
        axis=0,
    ).astype(jnp.bfloat16)
    cut = jnp.dot(place, table, preferred_element_type=jnp.float32)
    for k in range(K_MAX):
        mine = cut[k * OWNERS : (k + 1) * OWNERS]
        for u in range(2):
            window = jnp.where(
                later[k],
                mine[:, u * LANES : (u + 1) * LANES],
                mine[:, 256 + u * LANES : 256 + (u + 1) * LANES],
            )
            wide[pl.ds(2 * k + u, OWNERS, stride=ROWS), :] = window
    shard = wide[pl.ds(15, OWNERS, stride=ROWS), :]
    wide[pl.ds(10, OWNERS, stride=ROWS), :] = jnp.where(
        low_half,
        pltpu.roll(shard, 1, 0),
        pltpu.roll(pltpu.roll(shard, OWNERS - 1, 0), WIN, 1),
    )
    sent[...] = wide[...].reshape(OWNERS, ROWS, LANES).astype(jnp.bfloat16)
    for r in range(4):
        for h in range(16):
            residual[0, r : r + 1, h * LANES : (h + 1) * LANES] = resid[
                r * 16 + h : r * 16 + h + 1, :
            ]


def total_variation(image, before, after, is_first, is_last):
    lane = lane_iota((8, LANES))
    row = lax.broadcasted_iota(jnp.int32, (8, LANES), 0)
    last_x = (lane == LANES - 1) & ((row & 3) == 3)
    first_x = (lane == 0) & ((row & 3) == 0)

    def units(here, ahead, no_step):
        step_z = jnp.where(no_step, 0.0, ahead - here)
        step_y = jnp.where(row >= 4, 0.0, pltpu.roll(here, 4, 0) - here)
        moved = pltpu.roll(here, LANES - 1, 1)
        moved = jnp.where(lane == LANES - 1, pltpu.roll(moved, 7, 0), moved)
        step_x = jnp.where(last_x, 0.0, moved - here)
        magnitude = jnp.sqrt(step_z * step_z + step_y * step_y + step_x * step_x + TV_EPS)
        return step_z / magnitude, step_y / magnitude, step_x / magnitude

    unit_z, unit_y, unit_x = units(image, after, is_last)
    below_z, _, _ = units(before, image, is_first)
    result = below_z - unit_z
    result = result + (jnp.where(row < 4, 0.0, pltpu.roll(unit_y, 4, 0)) - unit_y)
    moved = pltpu.roll(unit_x, 1, 1)
    moved = jnp.where(lane == 0, pltpu.roll(moved, 1, 0), moved)
    return result + (jnp.where(first_x, 0.0, moved) - unit_x)


def smooth_kernel(got, image, base, wide):
    vox = lax.axis_index(VOX)
    wide[...] = got[:, 8:16, :].astype(jnp.float32).reshape(OWNERS * 8, LANES)
    shard = wide[pl.ds(2, OWNERS, stride=8), :]
    whole = shard + (pltpu.roll(shard, LANES - 8, 1) + pltpu.roll(shard, LANES - 16, 1))
    turned = jnp.concatenate([whole, pltpu.roll(whole, LANES - 24, 1)], axis=0).T
    here = as_tile(image)
    tv = total_variation(here, turned[0:8], turned[64:72], vox == 0, vox == OWNERS - 1)
    out = here - (STEP_SIZE * TV_WEIGHT) * tv
    for y in range(2):
        for t in range(4):
            base[0, y : y + 1, t * LANES : (t + 1) * LANES] = out[y * 4 + t : y * 4 + t + 1]


def backward_kernel(ids, starts, counts, got, held, grad, wins):
    live = counts[0, 0]
    lane = lane_iota((8, LANES))
    for k in range(K_MAX):
        block = ids[0, 0, k]
        for q in range(4):
            strip = got[4 * block + q].astype(jnp.float32)
            wins[k, 2 * q : 2 * q + 2, :] = strip[2 * k : 2 * k + 2, :]
    windows = []
    for k in range(K_MAX):
        low = lax.rem(starts[0, 0, k], WIN)
        tile = wins[k]
        tile = jnp.where(
            (lane & (WIN - 1)) < WIN - low,
            pltpu.roll(tile, lax.rem(LANES - low, LANES), 1),
            pltpu.roll(tile, WIN - low, 1),
        )
        windows.append(jnp.where(k < live, tile, 0.0))
    vectors = [
        jnp.concatenate([windows[k][i : i + 1, :] for i in range(8)], axis=1).astype(jnp.bfloat16)
        for k in range(ON_MATRIX)
    ]
    for j in range(8):
        rows = slice(j * LANES, (j + 1) * LANES)
        total = jnp.zeros((1, LANES), jnp.float32)
        for k in range(ON_MATRIX):
            total = total + lax.dot_general(
                vectors[k],
                held[k, rows, :],
                (((1,), (1,)), ((), ())),
                preferred_element_type=jnp.float32,
            )
        partial = jnp.zeros((LANES, LANES), jnp.float32)
        for k in range(ON_MATRIX, K_MAX):
            block = held[k, rows, :].astype(jnp.float32)
            for i in range(8):
                weight = jnp.broadcast_to(windows[k][i : i + 1, :], (LANES, LANES))
                partial = partial + block[:, i * LANES : (i + 1) * LANES] * weight
        total = total + jnp.sum(partial.T, axis=0, keepdims=True)
        y, t = j // 4, j % 4
        grad[0, y : y + 1, t * LANES : (t + 1) * LANES] = total


def smem():
    return pl.BlockSpec(memory_space=pltpu.SMEM)


def vmem():
    return pl.BlockSpec(memory_space=pltpu.VMEM)


def hbm():
    return pl.BlockSpec(memory_space=pltpu.HBM)


def in_hbm(array):
    return pltpu.with_memory_space_constraint(array, pltpu.HBM)


def on_device(image, weights, block_ids, offsets, counts, measured):
    sent, spread, held = pl.pallas_call(
        forward_kernel,
        out_shape=(
            jax.ShapeDtypeStruct((OWNERS, ROWS, LANES), jnp.bfloat16),
            jax.ShapeDtypeStruct((64, LANES), jnp.float32),
            jax.ShapeDtypeStruct((K_MAX, VOXELS, CELLS), jnp.bfloat16),
        ),
        in_specs=[hbm(), hbm(), smem(), hbm(), hbm(), hbm()],
        out_specs=(vmem(), vmem(), vmem()),
        scratch_shapes=[
            pltpu.SMEM((1, 1, K_MAX), jnp.int32),
            pltpu.SMEM((1, 1, K_MAX), jnp.int32),
            pltpu.VMEM((1, 2, 512), jnp.float32),
            pltpu.VMEM((1, 4, 2048), jnp.bfloat16),
            pltpu.VMEM((4, ROWS, LANES), jnp.float32),
            pltpu.VMEM((OWNERS, LANES), jnp.float32),
            pltpu.SemaphoreType.DMA((4,)),
            pltpu.SemaphoreType.DMA((K_MAX,)),
        ],
        compiler_params=pltpu.CompilerParams(vmem_limit_bytes=20 * MIB),
        name="forward",
    )(
        in_hbm(block_ids),
        in_hbm(offsets),
        counts,
        in_hbm(image),
        in_hbm(weights),
        in_hbm(measured),
    )
    got = lax.all_to_all(sent, VOX, 0, 0, tiled=True)
    sent, residual = pl.pallas_call(
        owner_kernel,
        out_shape=(
            jax.ShapeDtypeStruct((OWNERS, ROWS, LANES), jnp.bfloat16),
            jax.ShapeDtypeStruct((1, 4, 2048), jnp.float32),
        ),
        in_specs=[vmem(), vmem()],
        out_specs=(vmem(), vmem()),
        scratch_shapes=[pltpu.VMEM((OWNERS * ROWS, LANES), jnp.float32)],
        compiler_params=pltpu.CompilerParams(vmem_limit_bytes=8 * MIB),
        name="owner",
    )(got, spread)
    got = lax.all_to_all(sent, VOX, 0, 0, tiled=True)
    grad = pl.pallas_call(
        backward_kernel,
        out_shape=jax.ShapeDtypeStruct((1, 2, 512), jnp.float32),
        in_specs=[smem(), smem(), smem(), vmem(), vmem()],
        out_specs=vmem(),
        scratch_shapes=[pltpu.VMEM((K_MAX, 8, LANES), jnp.float32)],
        compiler_params=pltpu.CompilerParams(vmem_limit_bytes=20 * MIB),
        name="backward",
    )(block_ids, offsets, counts, got, held)
    grad = grad + lax.ppermute(grad, "core", [(0, 1), (1, 0)])
    other = lax.ppermute(grad, "z_hi", [(0, 1), (1, 0)])
    base = pl.pallas_call(
        smooth_kernel,
        out_shape=jax.ShapeDtypeStruct((1, 2, 512), jnp.float32),
        in_specs=[vmem(), vmem()],
        out_specs=vmem(),
        scratch_shapes=[pltpu.VMEM((OWNERS * 8, LANES), jnp.float32)],
        compiler_params=pltpu.CompilerParams(vmem_limit_bytes=8 * MIB),
        cost_estimate=pl.CostEstimate(flops=100000, bytes_accessed=1 << 19, transcendentals=4096),
        name="smooth",
    )(got, image)
    return (base - STEP_SIZE * (grad + other), residual)


def solution(mesh):
    fine = Mesh(mesh.devices.reshape(4, 4, 4, 2, 2), VOX + SEN)
    placed = (
        P(VOX, None, None),
        P(VOX, SEN, None, None, None),
        P(VOX, SEN, None),
        P(VOX, SEN, None),
        P(VOX, SEN),
        P(SEN, VOX, None),
    )
    return jax.shard_map(
        on_device,
        mesh=fine,
        in_specs=placed,
        out_specs=(P(VOX, None, None), P(SEN, VOX, None)),
        check_vma=False,
    )
```

```python
import functools

import jax
import jax.numpy as jnp
from jax import lax
from jax.experimental import pallas as pl
from jax.experimental.pallas import tpu as pltpu
from jax.sharding import Mesh
from jax.sharding import PartitionSpec as P

SB = 16
WIN = 64
K_MAX = 5
VOXELS = 1024
CELLS = SB * WIN
LANES = 128
TILES = K_MAX + 1
WIDTH = TILES * LANES
OWNERS = 64
ON_MATRIX = 2
IN_FLIGHT = 3
STEP_SIZE = 0.25
TV_WEIGHT = 0.3
TV_EPS = 0.01
NOWHERE = 255.0
MIB = 1 << 20

VOX = ("y", "x", "z_lo")
SEN = ("z_hi", "core")


def lane_iota(shape):
    return lax.broadcasted_iota(jnp.int32, shape, len(shape) - 1)


def as_tile(image):
    rows = [image[0, y : y + 1, t * LANES : (t + 1) * LANES] for y in range(2) for t in range(4)]
    return jnp.concatenate(rows, axis=0)


def split_three(x):
    parts = []
    for _ in range(3):
        part = x.astype(jnp.bfloat16).astype(jnp.float32)
        parts.append(part)
        x = x - part
    return parts


def forward_kernel(
    ids_hbm,
    starts_hbm,
    counts,
    image_hbm,
    weights,
    measured_hbm,
    sent,
    spread,
    held,
    ids,
    starts,
    image,
    measured,
    halo,
    small_sems,
    sems,
):
    small = []
    for i, (src, dst) in enumerate(
        (
            (image_hbm, image),
            (ids_hbm, ids),
            (starts_hbm, starts),
            (measured_hbm, measured),
        )
    ):
        small.append(pltpu.make_async_copy(src, dst, small_sems.at[i]))
        small[-1].start()
    copies = [
        pltpu.make_async_copy(weights.at[0, 0, k], held.at[k], sems.at[k]) for k in range(K_MAX)
    ]
    for copy in copies[:IN_FLIGHT]:
        copy.start()
    for copy in small:
        copy.wait()

    own = measured[0].astype(jnp.float32)
    for r in range(4):
        for h in range(16):
            spread[r * 16 + h : r * 16 + h + 1, :] = own[r : r + 1, h * LANES : (h + 1) * LANES]

    plane = as_tile(image)
    turned = jnp.concatenate(split_three(plane) + [jnp.zeros((104, LANES), jnp.float32)], axis=0).T
    halo[...] = pltpu.roll(turned, 32, 1)

    voxels = jnp.concatenate([image[0, 0:1, :], image[0, 1:2, :]], axis=1).astype(jnp.bfloat16)
    lane2 = lane_iota((2, LANES))
    base = jnp.full((2, LANES), NOWHERE, jnp.float32)
    code_row = base
    block_row = jnp.full((2, LANES), -1, jnp.int32)
    live = counts[0, 0]
    for k in range(K_MAX):
        start = starts[0, 0, k]
        coarse = start // WIN
        low = start - coarse * WIN
        code = (coarse & 1) * 16 + (coarse >> 1)
        block = jnp.where(k < live, ids[0, 0, k], -1)
        base = jnp.where(lane2 == 8 + k, low.astype(jnp.float32), base)
        code_row = jnp.where(lane2 == k, code.astype(jnp.float32), code_row)
        block_row = jnp.where(lane2 == k, block, block_row)
    for b in range(16):
        marked = jnp.where(block_row == b, code_row, base)
        for d in range(4 * b, 4 * b + 4):
            own_halo = halo[pl.ds(d, 2, stride=OWNERS), :]
            sent[d, :, K_MAX * LANES :] = jnp.where(lane2 < 32, marked, own_halo).astype(
                jnp.bfloat16
            )

    lane = lane_iota((8, LANES))
    for k in range(K_MAX):
        copies[k].wait()
        if k + IN_FLIGHT < K_MAX:
            copies[k + IN_FLIGHT].start()
        piece = jnp.dot(voxels, held[k], preferred_element_type=jnp.float32)
        tile = jnp.concatenate([piece[:, i * LANES : (i + 1) * LANES] for i in range(8)], axis=0)
        low = lax.rem(starts[0, 0, k], WIN)
        tile = jnp.where(
            (lane & (WIN - 1)) >= low, pltpu.roll(tile, low, 1), pltpu.roll(tile, low + WIN, 1)
        )
        for q in range(4):
            strip = tile[2 * q : 2 * q + 2, :].astype(jnp.bfloat16)
            for b in range(16):
                sent[4 * b + q, :, k * LANES : (k + 1) * LANES] = strip


def derivative(x):
    row = lax.broadcasted_iota(jnp.int32, x.shape, 0) & 15
    lane = lane_iota(x.shape)

    def ahead(t):
        rolled = pltpu.roll(x, LANES - t, 1)
        after = jnp.where(row == 15, 0.0, pltpu.roll(rolled, x.shape[0] - 1, 0))
        return jnp.where(lane >= LANES - t, after, rolled)

    def behind(t):
        rolled = pltpu.roll(x, t, 1)
        before = jnp.where(row == 0, 0.0, pltpu.roll(rolled, 1, 0))
        return jnp.where(lane < t, before, rolled)

    return ((behind(2) - ahead(2)) + 8.0 * (ahead(1) - behind(1))) * (1.0 / 12.0)


def owner_kernel(got, spread, sent, residual, wide):
    for d in range(OWNERS):
        wide[2 * d : 2 * d + 2, :] = got[d].astype(jnp.float32)
    lane = lane_iota((LANES, LANES))
    parity = lax.broadcasted_iota(jnp.int32, (LANES, LANES), 0) & 1
    within = (lane & (WIN - 1)).astype(jnp.float32)
    own_half = (lane >> 6) == parity
    first_half = (lane & 32) == 0
    slot = jnp.where(own_half, lane & 31, -1).astype(jnp.float32)
    info = wide[:, K_MAX * LANES :]
    places, strips, later = [], [], []
    for k in range(K_MAX):
        code = jnp.broadcast_to(info[:, k : k + 1], (LANES, LANES))
        low = jnp.broadcast_to(info[:, 8 + k : 9 + k], (LANES, LANES))
        following = jnp.where(code >= 16.0, code - 15.0, code + 16.0)
        wanted = jnp.where(first_half, code, following)
        places.append(jnp.where(wanted == slot, 1.0, 0.0))
        first = within >= low
        later.append(first)
        strip = wide[:, k * LANES : (k + 1) * LANES]
        strips.append(
            jnp.concatenate([jnp.where(first, strip, 0.0), jnp.where(first, 0.0, strip)], axis=1)
        )
    place = jnp.concatenate(places, axis=0).astype(jnp.bfloat16)
    strip = jnp.concatenate(strips, axis=0).astype(jnp.bfloat16)
    both = lax.dot_general(
        place, strip, (((0,), (0,)), ((), ())), preferred_element_type=jnp.float32
    )
    lane16 = lane_iota((16, LANES)) < WIN
    rows = []
    for u in range(2):
        summed = both[64 * u : 64 * u + 32, :LANES] + both[64 * u + 32 : 64 * u + 64, LANES:]
        even = summed[0:16]
        odd = summed[16:32]
        rows.append(jnp.where(lane16, even, pltpu.roll(odd, WIN, 1)))
        rows.append(jnp.where(lane16, pltpu.roll(even, WIN, 1), odd))
    signals = jnp.concatenate(rows, axis=0)
    resid = derivative(signals) - spread[...]
    adjoint = -derivative(resid)
    zero = jnp.zeros((32, LANES), jnp.float32)
    table = []
    for u in range(2):
        a = adjoint[32 * u : 32 * u + 16]
        b = adjoint[32 * u + 16 : 32 * u + 32]
        half = jnp.concatenate(
            [
                jnp.where(lane16, a, pltpu.roll(b, WIN, 1)),
                jnp.where(lane16, pltpu.roll(a, WIN, 1), b),
            ],
            axis=0,
        )
        table.append(jnp.concatenate([half, zero], axis=1))
        table.append(jnp.concatenate([zero, half], axis=1))
    table = jnp.concatenate(table, axis=0).astype(jnp.bfloat16)
    cut = jnp.dot(place, table, preferred_element_type=jnp.float32)
    for k in range(K_MAX):
        mine = cut[k * LANES : (k + 1) * LANES]
        wide[:, k * LANES : (k + 1) * LANES] = jnp.where(
            later[k], mine[:, :LANES], mine[:, LANES:]
        )
    wide[:, K_MAX * LANES :] = jnp.where(
        lane < WIN,
        pltpu.roll(info, 2, 0),
        pltpu.roll(pltpu.roll(info, LANES - 2, 0), 32, 1),
    )
    for d in range(OWNERS):
        sent[d] = wide[2 * d : 2 * d + 2, :].astype(jnp.bfloat16)
    for r in range(4):
        for h in range(16):
            residual[0, r : r + 1, h * LANES : (h + 1) * LANES] = resid[
                r * 16 + h : r * 16 + h + 1, :
            ]


def total_variation(image, before, after, is_first, is_last):
    lane = lane_iota((8, LANES))
    row = lax.broadcasted_iota(jnp.int32, (8, LANES), 0)
    last_x = (lane == LANES - 1) & ((row & 3) == 3)
    first_x = (lane == 0) & ((row & 3) == 0)

    def units(here, ahead, no_step):
        step_z = jnp.where(no_step, 0.0, ahead - here)
        step_y = jnp.where(row >= 4, 0.0, pltpu.roll(here, 4, 0) - here)
        moved = pltpu.roll(here, LANES - 1, 1)
        moved = jnp.where(lane == LANES - 1, pltpu.roll(moved, 7, 0), moved)
        step_x = jnp.where(last_x, 0.0, moved - here)
        magnitude = jnp.sqrt(step_z * step_z + step_y * step_y + step_x * step_x + TV_EPS)
        return step_z / magnitude, step_y / magnitude, step_x / magnitude

    unit_z, unit_y, unit_x = units(image, after, is_last)
    below_z, _, _ = units(before, image, is_first)
    result = below_z - unit_z
    result = result + (jnp.where(row < 4, 0.0, pltpu.roll(unit_y, 4, 0)) - unit_y)
    moved = pltpu.roll(unit_x, 1, 1)
    moved = jnp.where(lane == 0, pltpu.roll(moved, 1, 0), moved)
    return result + (jnp.where(first_x, 0.0, moved) - unit_x)


def smooth_kernel(got, image, base, wide):
    vox = lax.axis_index(VOX)
    for d in range(OWNERS):
        wide[2 * d : 2 * d + 2, :] = got[d, :, K_MAX * LANES :].astype(jnp.float32)
    shard = jnp.concatenate([wide[pl.ds(u, OWNERS, stride=2), :] for u in range(2)], axis=0)
    whole = shard + (pltpu.roll(shard, LANES - 8, 1) + pltpu.roll(shard, LANES - 16, 1))
    turned = whole.T
    here = as_tile(image)
    tv = total_variation(here, turned[32:40], turned[64:72], vox == 0, vox == OWNERS - 1)
    out = here - (STEP_SIZE * TV_WEIGHT) * tv
    for y in range(2):
        for t in range(4):
            base[0, y : y + 1, t * LANES : (t + 1) * LANES] = out[y * 4 + t : y * 4 + t + 1]


def backward_kernel(ids, starts, counts, got, held, grad, wins):
    live = counts[0, 0]
    lane = lane_iota((8, LANES))
    for k in range(K_MAX):
        block = ids[0, 0, k]
        for q in range(4):
            strip = got[4 * block + q, :, k * LANES : (k + 1) * LANES]
            wins[k, 2 * q : 2 * q + 2, :] = strip.astype(jnp.float32)
    windows = []
    for k in range(K_MAX):
        low = lax.rem(starts[0, 0, k], WIN)
        tile = wins[k]
        tile = jnp.where(
            (lane & (WIN - 1)) < WIN - low,
            pltpu.roll(tile, lax.rem(LANES - low, LANES), 1),
            pltpu.roll(tile, WIN - low, 1),
        )
        windows.append(jnp.where(k < live, tile, 0.0))
    vectors = [
        jnp.concatenate([windows[k][i : i + 1, :] for i in range(8)], axis=1).astype(jnp.bfloat16)
        for k in range(ON_MATRIX)
    ]
    for j in range(8):
        rows = slice(j * LANES, (j + 1) * LANES)
        total = jnp.zeros((1, LANES), jnp.float32)
        for k in range(ON_MATRIX):
            total = total + lax.dot_general(
                vectors[k],
                held[k, rows, :],
                (((1,), (1,)), ((), ())),
                preferred_element_type=jnp.float32,
            )
        partial = jnp.zeros((LANES, LANES), jnp.float32)
        for k in range(ON_MATRIX, K_MAX):
            block = held[k, rows, :].astype(jnp.float32)
            for i in range(8):
                weight = jnp.broadcast_to(windows[k][i : i + 1, :], (LANES, LANES))
                partial = partial + block[:, i * LANES : (i + 1) * LANES] * weight
        total = total + jnp.sum(partial.T, axis=0, keepdims=True)
        y, t = j // 4, j % 4
        grad[0, y : y + 1, t * LANES : (t + 1) * LANES] = total


def smem():
    return pl.BlockSpec(memory_space=pltpu.SMEM)


def vmem():
    return pl.BlockSpec(memory_space=pltpu.VMEM)


def hbm():
    return pl.BlockSpec(memory_space=pltpu.HBM)


def in_hbm(array):
    return pltpu.with_memory_space_constraint(array, pltpu.HBM)


def on_device(image, weights, block_ids, offsets, counts, measured):
    sent, spread, held = pl.pallas_call(
        forward_kernel,
        out_shape=(
            jax.ShapeDtypeStruct((OWNERS, 2, WIDTH), jnp.bfloat16),
            jax.ShapeDtypeStruct((64, LANES), jnp.float32),
            jax.ShapeDtypeStruct((K_MAX, VOXELS, CELLS), jnp.bfloat16),
        ),
        in_specs=[hbm(), hbm(), smem(), hbm(), hbm(), hbm()],
        out_specs=(vmem(), vmem(), vmem()),
        scratch_shapes=[
            pltpu.SMEM((1, 1, K_MAX), jnp.int32),
            pltpu.SMEM((1, 1, K_MAX), jnp.int32),
            pltpu.VMEM((1, 2, 512), jnp.float32),
            pltpu.VMEM((1, 4, 2048), jnp.bfloat16),
            pltpu.VMEM((2 * OWNERS, LANES), jnp.float32),
            pltpu.SemaphoreType.DMA((4,)),
            pltpu.SemaphoreType.DMA((K_MAX,)),
        ],
        compiler_params=pltpu.CompilerParams(vmem_limit_bytes=20 * MIB),
        name="forward",
    )(
        in_hbm(block_ids),
        in_hbm(offsets),
        counts,
        in_hbm(image),
        in_hbm(weights),
        in_hbm(measured),
    )
    got = lax.all_to_all(sent, VOX, 0, 0, tiled=True)
    sent, residual = pl.pallas_call(
        owner_kernel,
        out_shape=(
            jax.ShapeDtypeStruct((OWNERS, 2, WIDTH), jnp.bfloat16),
            jax.ShapeDtypeStruct((1, 4, 2048), jnp.float32),
        ),
        in_specs=[vmem(), vmem()],
        out_specs=(vmem(), vmem()),
        scratch_shapes=[pltpu.VMEM((2 * OWNERS, WIDTH), jnp.float32)],
        compiler_params=pltpu.CompilerParams(vmem_limit_bytes=8 * MIB),
        name="owner",
    )(got, spread)
    got = lax.all_to_all(sent, VOX, 0, 0, tiled=True)
    grad = pl.pallas_call(
        backward_kernel,
        out_shape=jax.ShapeDtypeStruct((1, 2, 512), jnp.float32),
        in_specs=[smem(), smem(), smem(), vmem(), vmem()],
        out_specs=vmem(),
        scratch_shapes=[pltpu.VMEM((K_MAX, 8, LANES), jnp.float32)],
        compiler_params=pltpu.CompilerParams(vmem_limit_bytes=20 * MIB),
        name="backward",
    )(block_ids, offsets, counts, got, held)
    grad = grad + lax.ppermute(grad, "core", [(0, 1), (1, 0)])
    other = lax.ppermute(grad, "z_hi", [(0, 1), (1, 0)])
    base = pl.pallas_call(
        smooth_kernel,
        out_shape=jax.ShapeDtypeStruct((1, 2, 512), jnp.float32),
        in_specs=[vmem(), vmem()],
        out_specs=vmem(),
        scratch_shapes=[pltpu.VMEM((2 * OWNERS, LANES), jnp.float32)],
        compiler_params=pltpu.CompilerParams(vmem_limit_bytes=8 * MIB),
        cost_estimate=pl.CostEstimate(flops=100000, bytes_accessed=1 << 19, transcendentals=4096),
        name="smooth",
    )(got, image)
    return (base - STEP_SIZE * (grad + other), residual)


def solution(mesh):
    fine = Mesh(mesh.devices.reshape(4, 4, 4, 2, 2), VOX + SEN)
    placed = (
        P(VOX, None, None),
        P(VOX, SEN, None, None, None),
        P(VOX, SEN, None),
        P(VOX, SEN, None),
        P(VOX, SEN),
        P(SEN, VOX, None),
    )
    return jax.shard_map(
        on_device,
        mesh=fine,
        in_specs=placed,
        out_specs=(P(VOX, None, None), P(SEN, VOX, None)),
        check_vma=False,
    )
```

```python
import functools

import jax
import jax.numpy as jnp
from jax import lax
from jax.experimental import pallas as pl
from jax.experimental.pallas import tpu as pltpu
from jax.sharding import Mesh
from jax.sharding import PartitionSpec as P

SB = 16
WIN = 64
K_MAX = 5
VOXELS = 1024
CELLS = SB * WIN
LANES = 128
TILES = K_MAX + 1
WIDTH = TILES * LANES
OWNERS = 64
ON_MATRIX = 2
IN_FLIGHT = 3
PLACE = 2048
LIVE = 16 * PLACE
STEP_SIZE = 0.25
TV_WEIGHT = 0.3
TV_EPS = 0.01
NOWHERE = 255.0
MIB = 1 << 20

VOX = ("y", "x", "z_lo")
SEN = ("z_hi", "core")


def lane_iota(shape):
    return lax.broadcasted_iota(jnp.int32, shape, len(shape) - 1)


def as_tile(image):
    rows = [image[0, y : y + 1, t * LANES : (t + 1) * LANES] for y in range(2) for t in range(4)]
    return jnp.concatenate(rows, axis=0)


def split_three(x):
    parts = []
    for _ in range(3):
        part = x.astype(jnp.bfloat16).astype(jnp.float32)
        parts.append(part)
        x = x - part
    return parts


def forward_kernel(
    ids_hbm,
    starts_hbm,
    counts,
    image_hbm,
    weights,
    measured_hbm,
    sent,
    spread,
    held,
    places,
    ids,
    starts,
    image,
    measured,
    halo,
    small_sems,
    sems,
):
    small = []
    for i, (src, dst) in enumerate(
        (
            (image_hbm, image),
            (ids_hbm, ids),
            (starts_hbm, starts),
            (measured_hbm, measured),
        )
    ):
        small.append(pltpu.make_async_copy(src, dst, small_sems.at[i]))
        small[-1].start()
    copies = [
        pltpu.make_async_copy(weights.at[0, 0, k], held.at[k], sems.at[k]) for k in range(K_MAX)
    ]
    for copy in copies[:IN_FLIGHT]:
        copy.start()
    for copy in small:
        copy.wait()

    own = measured[0].astype(jnp.float32)
    for r in range(4):
        for h in range(16):
            spread[r * 16 + h : r * 16 + h + 1, :] = own[r : r + 1, h * LANES : (h + 1) * LANES]

    plane = as_tile(image)
    turned = jnp.concatenate(split_three(plane) + [jnp.zeros((104, LANES), jnp.float32)], axis=0).T
    halo[...] = pltpu.roll(turned, 32, 1)

    voxels = jnp.concatenate([image[0, 0:1, :], image[0, 1:2, :]], axis=1).astype(jnp.bfloat16)
    lane2 = lane_iota((2, LANES))
    base = jnp.full((2, LANES), NOWHERE, jnp.float32)
    code_row = base
    block_row = jnp.full((2, LANES), -1, jnp.int32)
    live = counts[0, 0]
    table = jnp.zeros((8, LANES), jnp.int32)
    for k in range(K_MAX):
        start = starts[0, 0, k]
        place = start + ids[0, 0, k] * PLACE + jnp.where(k < live, LIVE, 0)
        table = jnp.where(lane_iota((8, LANES)) == k, place, table)
        coarse = start // WIN
        low = start - coarse * WIN
        code = (coarse & 1) * 16 + (coarse >> 1)
        block = jnp.where(k < live, ids[0, 0, k], -1)
        base = jnp.where(lane2 == 8 + k, low.astype(jnp.float32), base)
        code_row = jnp.where(lane2 == k, code.astype(jnp.float32), code_row)
        block_row = jnp.where(lane2 == k, block, block_row)
    places[...] = table
    for b in range(16):
        marked = jnp.where(block_row == b, code_row, base)
        for d in range(4 * b, 4 * b + 4):
            own_halo = halo[pl.ds(d, 2, stride=OWNERS), :]
            sent[d, :, K_MAX * LANES :] = jnp.where(lane2 < 32, marked, own_halo).astype(
                jnp.bfloat16
            )

    lane = lane_iota((8, LANES))
    for k in range(K_MAX):
        copies[k].wait()
        if k + IN_FLIGHT < K_MAX:
            copies[k + IN_FLIGHT].start()
        piece = jnp.dot(voxels, held[k], preferred_element_type=jnp.float32)
        tile = jnp.concatenate([piece[:, i * LANES : (i + 1) * LANES] for i in range(8)], axis=0)
        low = lax.rem(starts[0, 0, k], WIN)
        tile = jnp.where(
            (lane & (WIN - 1)) >= low, pltpu.roll(tile, low, 1), pltpu.roll(tile, low + WIN, 1)
        )
        for q in range(4):
            strip = tile[2 * q : 2 * q + 2, :].astype(jnp.bfloat16)
            for b in range(16):
                sent[4 * b + q, :, k * LANES : (k + 1) * LANES] = strip


def derivative(x):
    row = lax.broadcasted_iota(jnp.int32, x.shape, 0) & 15
    lane = lane_iota(x.shape)

    def ahead(t):
        rolled = pltpu.roll(x, LANES - t, 1)
        after = jnp.where(row == 15, 0.0, pltpu.roll(rolled, x.shape[0] - 1, 0))
        return jnp.where(lane >= LANES - t, after, rolled)

    def behind(t):
        rolled = pltpu.roll(x, t, 1)
        before = jnp.where(row == 0, 0.0, pltpu.roll(rolled, 1, 0))
        return jnp.where(lane < t, before, rolled)

    return ((behind(2) - ahead(2)) + 8.0 * (ahead(1) - behind(1))) * (1.0 / 12.0)


def owner_kernel(got, spread, sent, resid, wide):
    for d in range(OWNERS):
        wide[2 * d : 2 * d + 2, :] = got[d].astype(jnp.float32)
    lane = lane_iota((LANES, LANES))
    parity = lax.broadcasted_iota(jnp.int32, (LANES, LANES), 0) & 1
    within = (lane & (WIN - 1)).astype(jnp.float32)
    own_half = (lane >> 6) == parity
    first_half = (lane & 32) == 0
    slot = jnp.where(own_half, lane & 31, -1).astype(jnp.float32)
    info = wide[:, K_MAX * LANES :]
    places, strips, later = [], [], []
    for k in range(K_MAX):
        code = jnp.broadcast_to(info[:, k : k + 1], (LANES, LANES))
        low = jnp.broadcast_to(info[:, 8 + k : 9 + k], (LANES, LANES))
        following = jnp.where(code >= 16.0, code - 15.0, code + 16.0)
        wanted = jnp.where(first_half, code, following)
        places.append(jnp.where(wanted == slot, 1.0, 0.0))
        first = within >= low
        later.append(first)
        strip = wide[:, k * LANES : (k + 1) * LANES]
        strips.append(
            jnp.concatenate([jnp.where(first, strip, 0.0), jnp.where(first, 0.0, strip)], axis=1)
        )
    place = jnp.concatenate(places, axis=0).astype(jnp.bfloat16)
    strip = jnp.concatenate(strips, axis=0).astype(jnp.bfloat16)
    both = lax.dot_general(
        place, strip, (((0,), (0,)), ((), ())), preferred_element_type=jnp.float32
    )
    lane16 = lane_iota((16, LANES)) < WIN
    rows = []
    for u in range(2):
        summed = both[64 * u : 64 * u + 32, :LANES] + both[64 * u + 32 : 64 * u + 64, LANES:]
        even = summed[0:16]
        odd = summed[16:32]
        rows.append(jnp.where(lane16, even, pltpu.roll(odd, WIN, 1)))
        rows.append(jnp.where(lane16, pltpu.roll(even, WIN, 1), odd))
    signals = jnp.concatenate(rows, axis=0)
    difference = derivative(signals) - spread[...]
    resid[...] = difference
    adjoint = -derivative(difference)
    zero = jnp.zeros((32, LANES), jnp.float32)
    table = []
    for u in range(2):
        a = adjoint[32 * u : 32 * u + 16]
        b = adjoint[32 * u + 16 : 32 * u + 32]
        half = jnp.concatenate(
            [
                jnp.where(lane16, a, pltpu.roll(b, WIN, 1)),
                jnp.where(lane16, pltpu.roll(a, WIN, 1), b),
            ],
            axis=0,
        )
        table.append(jnp.concatenate([half, zero], axis=1))
        table.append(jnp.concatenate([zero, half], axis=1))
    table = jnp.concatenate(table, axis=0).astype(jnp.bfloat16)
    cut = jnp.dot(place, table, preferred_element_type=jnp.float32)
    for k in range(K_MAX):
        mine = cut[k * LANES : (k + 1) * LANES]
        wide[:, k * LANES : (k + 1) * LANES] = jnp.where(
            later[k], mine[:, :LANES], mine[:, LANES:]
        )
    wide[:, K_MAX * LANES :] = jnp.where(
        lane < WIN,
        pltpu.roll(info, 2, 0),
        pltpu.roll(pltpu.roll(info, LANES - 2, 0), 32, 1),
    )
    for d in range(OWNERS):
        sent[d] = wide[2 * d : 2 * d + 2, :].astype(jnp.bfloat16)


def total_variation(image, before, after, is_first, is_last):
    lane = lane_iota((8, LANES))
    row = lax.broadcasted_iota(jnp.int32, (8, LANES), 0)
    last_x = (lane == LANES - 1) & ((row & 3) == 3)
    first_x = (lane == 0) & ((row & 3) == 0)

    def units(here, ahead, no_step):
        step_z = jnp.where(no_step, 0.0, ahead - here)
        step_y = jnp.where(row >= 4, 0.0, pltpu.roll(here, 4, 0) - here)
        moved = pltpu.roll(here, LANES - 1, 1)
        moved = jnp.where(lane == LANES - 1, pltpu.roll(moved, 7, 0), moved)
        step_x = jnp.where(last_x, 0.0, moved - here)
        magnitude = jnp.sqrt(step_z * step_z + step_y * step_y + step_x * step_x + TV_EPS)
        return step_z / magnitude, step_y / magnitude, step_x / magnitude

    unit_z, unit_y, unit_x = units(image, after, is_last)
    below_z, _, _ = units(before, image, is_first)
    result = below_z - unit_z
    result = result + (jnp.where(row < 4, 0.0, pltpu.roll(unit_y, 4, 0)) - unit_y)
    moved = pltpu.roll(unit_x, 1, 1)
    moved = jnp.where(lane == 0, pltpu.roll(moved, 1, 0), moved)
    return result + (jnp.where(first_x, 0.0, moved) - unit_x)


def smooth_kernel(got, image, resid, base, residual, wide):
    for r in range(4):
        for h in range(16):
            residual[0, r : r + 1, h * LANES : (h + 1) * LANES] = resid[
                r * 16 + h : r * 16 + h + 1, :
            ]
    vox = lax.axis_index(VOX)
    for d in range(OWNERS):
        wide[2 * d : 2 * d + 2, :] = got[d, :, K_MAX * LANES :].astype(jnp.float32)
    shard = jnp.concatenate([wide[pl.ds(u, OWNERS, stride=2), :] for u in range(2)], axis=0)
    whole = shard + (pltpu.roll(shard, LANES - 8, 1) + pltpu.roll(shard, LANES - 16, 1))
    turned = whole.T
    here = as_tile(image)
    tv = total_variation(here, turned[32:40], turned[64:72], vox == 0, vox == OWNERS - 1)
    out = here - (STEP_SIZE * TV_WEIGHT) * tv
    for y in range(2):
        for t in range(4):
            base[0, y : y + 1, t * LANES : (t + 1) * LANES] = out[y * 4 + t : y * 4 + t + 1]


def backward_kernel(table, got, held, grad, wins):
    lane = lane_iota((8, LANES))
    places = [table[0, k] for k in range(K_MAX)]
    for k in range(K_MAX):
        block = (places[k] >> 11) & 15
        for q in range(4):
            strip = got[4 * block + q, :, k * LANES : (k + 1) * LANES]
            wins[k, 2 * q : 2 * q + 2, :] = strip.astype(jnp.float32)
    windows = []
    for k in range(K_MAX):
        low = places[k] & (WIN - 1)
        tile = wins[k]
        tile = jnp.where(
            (lane & (WIN - 1)) < WIN - low,
            pltpu.roll(tile, lax.rem(LANES - low, LANES), 1),
            pltpu.roll(tile, WIN - low, 1),
        )
        windows.append(jnp.where(places[k] >= LIVE, tile, 0.0))
    vectors = [
        jnp.concatenate([windows[k][i : i + 1, :] for i in range(8)], axis=1).astype(jnp.bfloat16)
        for k in range(ON_MATRIX)
    ]
    for j in range(8):
        rows = slice(j * LANES, (j + 1) * LANES)
        total = jnp.zeros((1, LANES), jnp.float32)
        for k in range(ON_MATRIX):
            total = total + lax.dot_general(
                vectors[k],
                held[k, rows, :],
                (((1,), (1,)), ((), ())),
                preferred_element_type=jnp.float32,
            )
        partial = jnp.zeros((LANES, LANES), jnp.float32)
        for k in range(ON_MATRIX, K_MAX):
            block = held[k, rows, :].astype(jnp.float32)
            for i in range(8):
                weight = jnp.broadcast_to(windows[k][i : i + 1, :], (LANES, LANES))
                partial = partial + block[:, i * LANES : (i + 1) * LANES] * weight
        total = total + jnp.sum(partial.T, axis=0, keepdims=True)
        y, t = j // 4, j % 4
        grad[0, y : y + 1, t * LANES : (t + 1) * LANES] = total


def smem():
    return pl.BlockSpec(memory_space=pltpu.SMEM)


def vmem():
    return pl.BlockSpec(memory_space=pltpu.VMEM)


def hbm():
    return pl.BlockSpec(memory_space=pltpu.HBM)


def in_hbm(array):
    return pltpu.with_memory_space_constraint(array, pltpu.HBM)


def on_device(image, weights, block_ids, offsets, counts, measured):
    sent, spread, held, places = pl.pallas_call(
        forward_kernel,
        out_shape=(
            jax.ShapeDtypeStruct((OWNERS, 2, WIDTH), jnp.bfloat16),
            jax.ShapeDtypeStruct((64, LANES), jnp.float32),
            jax.ShapeDtypeStruct((K_MAX, VOXELS, CELLS), jnp.bfloat16),
            jax.ShapeDtypeStruct((8, LANES), jnp.int32),
        ),
        in_specs=[hbm(), hbm(), smem(), hbm(), hbm(), hbm()],
        out_specs=(vmem(),) * 4,
        scratch_shapes=[
            pltpu.SMEM((1, 1, K_MAX), jnp.int32),
            pltpu.SMEM((1, 1, K_MAX), jnp.int32),
            pltpu.VMEM((1, 2, 512), jnp.float32),
            pltpu.VMEM((1, 4, 2048), jnp.bfloat16),
            pltpu.VMEM((2 * OWNERS, LANES), jnp.float32),
            pltpu.SemaphoreType.DMA((4,)),
            pltpu.SemaphoreType.DMA((K_MAX,)),
        ],
        compiler_params=pltpu.CompilerParams(vmem_limit_bytes=20 * MIB),
        name="forward",
    )(
        in_hbm(block_ids),
        in_hbm(offsets),
        counts,
        in_hbm(image),
        in_hbm(weights),
        in_hbm(measured),
    )
    got = lax.all_to_all(sent, VOX, 0, 0, tiled=True)
    sent, resid = pl.pallas_call(
        owner_kernel,
        out_shape=(
            jax.ShapeDtypeStruct((OWNERS, 2, WIDTH), jnp.bfloat16),
            jax.ShapeDtypeStruct((64, LANES), jnp.float32),
        ),
        in_specs=[vmem(), vmem()],
        out_specs=(vmem(), vmem()),
        scratch_shapes=[pltpu.VMEM((2 * OWNERS, WIDTH), jnp.float32)],
        compiler_params=pltpu.CompilerParams(vmem_limit_bytes=8 * MIB),
        name="owner",
    )(got, spread)
    got = lax.all_to_all(sent, VOX, 0, 0, tiled=True)
    grad = pl.pallas_call(
        backward_kernel,
        out_shape=jax.ShapeDtypeStruct((1, 2, 512), jnp.float32),
        in_specs=[vmem(), vmem(), vmem()],
        out_specs=vmem(),
        scratch_shapes=[pltpu.VMEM((K_MAX, 8, LANES), jnp.float32)],
        compiler_params=pltpu.CompilerParams(vmem_limit_bytes=20 * MIB),
        name="backward",
    )(places, got, held)
    grad = grad + lax.ppermute(grad, "core", [(0, 1), (1, 0)])
    other = lax.ppermute(grad, "z_hi", [(0, 1), (1, 0)])
    base, residual = pl.pallas_call(
        smooth_kernel,
        out_shape=(
            jax.ShapeDtypeStruct((1, 2, 512), jnp.float32),
            jax.ShapeDtypeStruct((1, 4, 2048), jnp.float32),
        ),
        in_specs=[vmem(), vmem(), vmem()],
        out_specs=(vmem(), vmem()),
        scratch_shapes=[pltpu.VMEM((2 * OWNERS, LANES), jnp.float32)],
        compiler_params=pltpu.CompilerParams(vmem_limit_bytes=8 * MIB),
        cost_estimate=pl.CostEstimate(flops=100000, bytes_accessed=1 << 19, transcendentals=4096),
        name="smooth",
    )(got, image, resid)
    return (base - STEP_SIZE * (grad + other), residual)


def solution(mesh):
    fine = Mesh(mesh.devices.reshape(4, 4, 4, 2, 2), VOX + SEN)
    placed = (
        P(VOX, None, None),
        P(VOX, SEN, None, None, None),
        P(VOX, SEN, None),
        P(VOX, SEN, None),
        P(VOX, SEN),
        P(SEN, VOX, None),
    )
    return jax.shard_map(
        on_device,
        mesh=fine,
        in_specs=placed,
        out_specs=(P(VOX, None, None), P(SEN, VOX, None)),
        check_vma=False,
    )
```

```python
import functools

import jax
import jax.numpy as jnp
from jax import lax
from jax.experimental import pallas as pl
from jax.experimental.pallas import tpu as pltpu
from jax.sharding import Mesh
from jax.sharding import PartitionSpec as P

SB = 16
WIN = 64
K_MAX = 5
VOXELS = 1024
CELLS = SB * WIN
LANES = 128
TILES = K_MAX + 1
WIDTH = TILES * LANES
OWNERS = 64
ON_MATRIX = 2
AHEAD = 2
PLACE = 2048
LIVE = 16 * PLACE
STEP_SIZE = 0.25
TV_WEIGHT = 0.3
TV_EPS = 0.01
NOWHERE = 255.0
MIB = 1 << 20

VOX = ("y", "x", "z_lo")
SEN = ("z_hi", "core")


def lane_iota(shape):
    return lax.broadcasted_iota(jnp.int32, shape, len(shape) - 1)


def as_tile(image):
    rows = [image[0, y : y + 1, t * LANES : (t + 1) * LANES] for y in range(2) for t in range(4)]
    return jnp.concatenate(rows, axis=0)


def split_three(x):
    parts = []
    for _ in range(3):
        part = x.astype(jnp.bfloat16).astype(jnp.float32)
        parts.append(part)
        x = x - part
    return parts


def forward_kernel(
    ids_hbm,
    starts_hbm,
    counts,
    image_hbm,
    weights,
    measured_hbm,
    sent,
    spread,
    held,
    places,
    ids,
    starts,
    image,
    measured,
    halo,
    small_sems,
    sems,
):
    small = []
    for i, (src, dst) in enumerate(
        (
            (image_hbm, image),
            (ids_hbm, ids),
            (starts_hbm, starts),
            (measured_hbm, measured),
        )
    ):
        small.append(pltpu.make_async_copy(src, dst, small_sems.at[i]))
        small[-1].start()
    copies = [
        pltpu.make_async_copy(weights.at[0, 0, k], held.at[k], sems.at[k]) for k in range(K_MAX)
    ]
    for k in range(K_MAX):
        copies[k].start(priority=0 if k < AHEAD else 1)
    for copy in small:
        copy.wait()

    own = measured[0].astype(jnp.float32)
    for r in range(4):
        for h in range(16):
            spread[r * 16 + h : r * 16 + h + 1, :] = own[r : r + 1, h * LANES : (h + 1) * LANES]

    plane = as_tile(image)
    turned = jnp.concatenate(split_three(plane) + [jnp.zeros((104, LANES), jnp.float32)], axis=0).T
    halo[...] = pltpu.roll(turned, 32, 1)

    voxels = jnp.concatenate([image[0, 0:1, :], image[0, 1:2, :]], axis=1).astype(jnp.bfloat16)
    lane2 = lane_iota((2, LANES))
    base = jnp.full((2, LANES), NOWHERE, jnp.float32)
    code_row = base
    block_row = jnp.full((2, LANES), -1, jnp.int32)
    live = counts[0, 0]
    table = jnp.zeros((8, LANES), jnp.int32)
    for k in range(K_MAX):
        start = starts[0, 0, k]
        place = start + ids[0, 0, k] * PLACE + jnp.where(k < live, LIVE, 0)
        table = jnp.where(lane_iota((8, LANES)) == k, place, table)
        coarse = start // WIN
        low = start - coarse * WIN
        code = (coarse & 1) * 16 + (coarse >> 1)
        block = jnp.where(k < live, ids[0, 0, k], -1)
        base = jnp.where(lane2 == 8 + k, low.astype(jnp.float32), base)
        code_row = jnp.where(lane2 == k, code.astype(jnp.float32), code_row)
        block_row = jnp.where(lane2 == k, block, block_row)
    places[...] = table
    for b in range(16):
        marked = jnp.where(block_row == b, code_row, base)
        for d in range(4 * b, 4 * b + 4):
            own_halo = halo[pl.ds(d, 2, stride=OWNERS), :]
            sent[d, :, K_MAX * LANES :] = jnp.where(lane2 < 32, marked, own_halo).astype(
                jnp.bfloat16
            )

    lane = lane_iota((8, LANES))
    for k in range(K_MAX):
        copies[k].wait()
        piece = jnp.dot(voxels, held[k], preferred_element_type=jnp.float32)
        tile = jnp.concatenate([piece[:, i * LANES : (i + 1) * LANES] for i in range(8)], axis=0)
        low = lax.rem(starts[0, 0, k], WIN)
        tile = jnp.where(
            (lane & (WIN - 1)) >= low, pltpu.roll(tile, low, 1), pltpu.roll(tile, low + WIN, 1)
        )
        for q in range(4):
            strip = tile[2 * q : 2 * q + 2, :].astype(jnp.bfloat16)
            for b in range(16):
                sent[4 * b + q, :, k * LANES : (k + 1) * LANES] = strip


def derivative(x):
    row = lax.broadcasted_iota(jnp.int32, x.shape, 0) & 15
    lane = lane_iota(x.shape)

    def ahead(t):
        rolled = pltpu.roll(x, LANES - t, 1)
        after = jnp.where(row == 15, 0.0, pltpu.roll(rolled, x.shape[0] - 1, 0))
        return jnp.where(lane >= LANES - t, after, rolled)

    def behind(t):
        rolled = pltpu.roll(x, t, 1)
        before = jnp.where(row == 0, 0.0, pltpu.roll(rolled, 1, 0))
        return jnp.where(lane < t, before, rolled)

    return ((behind(2) - ahead(2)) + 8.0 * (ahead(1) - behind(1))) * (1.0 / 12.0)


def owner_kernel(got, spread, sent, resid, wide):
    for d in range(OWNERS):
        wide[2 * d : 2 * d + 2, :] = got[d].astype(jnp.float32)
    lane = lane_iota((LANES, LANES))
    parity = lax.broadcasted_iota(jnp.int32, (LANES, LANES), 0) & 1
    within = (lane & (WIN - 1)).astype(jnp.float32)
    own_half = (lane >> 6) == parity
    first_half = (lane & 32) == 0
    slot = jnp.where(own_half, lane & 31, -1).astype(jnp.float32)
    info = wide[:, K_MAX * LANES :]
    places, strips, later = [], [], []
    for k in range(K_MAX):
        code = jnp.broadcast_to(info[:, k : k + 1], (LANES, LANES))
        low = jnp.broadcast_to(info[:, 8 + k : 9 + k], (LANES, LANES))
        following = jnp.where(code >= 16.0, code - 15.0, code + 16.0)
        wanted = jnp.where(first_half, code, following)
        places.append(jnp.where(wanted == slot, 1.0, 0.0))
        first = within >= low
        later.append(first)
        strip = wide[:, k * LANES : (k + 1) * LANES]
        strips.append(
            jnp.concatenate([jnp.where(first, strip, 0.0), jnp.where(first, 0.0, strip)], axis=1)
        )
    place = jnp.concatenate(places, axis=0).astype(jnp.bfloat16)
    strip = jnp.concatenate(strips, axis=0).astype(jnp.bfloat16)
    both = lax.dot_general(
        place, strip, (((0,), (0,)), ((), ())), preferred_element_type=jnp.float32
    )
    lane16 = lane_iota((16, LANES)) < WIN
    rows = []
    for u in range(2):
        summed = both[64 * u : 64 * u + 32, :LANES] + both[64 * u + 32 : 64 * u + 64, LANES:]
        even = summed[0:16]
        odd = summed[16:32]
        rows.append(jnp.where(lane16, even, pltpu.roll(odd, WIN, 1)))
        rows.append(jnp.where(lane16, pltpu.roll(even, WIN, 1), odd))
    signals = jnp.concatenate(rows, axis=0)
    difference = derivative(signals) - spread[...]
    resid[...] = difference
    adjoint = -derivative(difference)
    zero = jnp.zeros((32, LANES), jnp.float32)
    table = []
    for u in range(2):
        a = adjoint[32 * u : 32 * u + 16]
        b = adjoint[32 * u + 16 : 32 * u + 32]
        half = jnp.concatenate(
            [
                jnp.where(lane16, a, pltpu.roll(b, WIN, 1)),
                jnp.where(lane16, pltpu.roll(a, WIN, 1), b),
            ],
            axis=0,
        )
        table.append(jnp.concatenate([half, zero], axis=1))
        table.append(jnp.concatenate([zero, half], axis=1))
    table = jnp.concatenate(table, axis=0).astype(jnp.bfloat16)
    cut = jnp.dot(place, table, preferred_element_type=jnp.float32)
    for k in range(K_MAX):
        mine = cut[k * LANES : (k + 1) * LANES]
        wide[:, k * LANES : (k + 1) * LANES] = jnp.where(
            later[k], mine[:, :LANES], mine[:, LANES:]
        )
    wide[:, K_MAX * LANES :] = jnp.where(
        lane < WIN,
        pltpu.roll(info, 2, 0),
        pltpu.roll(pltpu.roll(info, LANES - 2, 0), 32, 1),
    )
    for d in range(OWNERS):
        sent[d] = wide[2 * d : 2 * d + 2, :].astype(jnp.bfloat16)


def total_variation(image, before, after, is_first, is_last):
    lane = lane_iota((8, LANES))
    row = lax.broadcasted_iota(jnp.int32, (8, LANES), 0)
    last_x = (lane == LANES - 1) & ((row & 3) == 3)
    first_x = (lane == 0) & ((row & 3) == 0)

    def units(here, ahead, no_step):
        step_z = jnp.where(no_step, 0.0, ahead - here)
        step_y = jnp.where(row >= 4, 0.0, pltpu.roll(here, 4, 0) - here)
        moved = pltpu.roll(here, LANES - 1, 1)
        moved = jnp.where(lane == LANES - 1, pltpu.roll(moved, 7, 0), moved)
        step_x = jnp.where(last_x, 0.0, moved - here)
        magnitude = jnp.sqrt(step_z * step_z + step_y * step_y + step_x * step_x + TV_EPS)
        return step_z / magnitude, step_y / magnitude, step_x / magnitude

    unit_z, unit_y, unit_x = units(image, after, is_last)
    below_z, _, _ = units(before, image, is_first)
    result = below_z - unit_z
    result = result + (jnp.where(row < 4, 0.0, pltpu.roll(unit_y, 4, 0)) - unit_y)
    moved = pltpu.roll(unit_x, 1, 1)
    moved = jnp.where(lane == 0, pltpu.roll(moved, 1, 0), moved)
    return result + (jnp.where(first_x, 0.0, moved) - unit_x)


def smooth_kernel(got, image, resid, base, residual, wide):
    for r in range(4):
        for h in range(16):
            residual[0, r : r + 1, h * LANES : (h + 1) * LANES] = resid[
                r * 16 + h : r * 16 + h + 1, :
            ]
    vox = lax.axis_index(VOX)
    for d in range(OWNERS):
        wide[2 * d : 2 * d + 2, :] = got[d, :, K_MAX * LANES :].astype(jnp.float32)
    shard = jnp.concatenate([wide[pl.ds(u, OWNERS, stride=2), :] for u in range(2)], axis=0)
    whole = shard + (pltpu.roll(shard, LANES - 8, 1) + pltpu.roll(shard, LANES - 16, 1))
    turned = whole.T
    here = as_tile(image)
    tv = total_variation(here, turned[32:40], turned[64:72], vox == 0, vox == OWNERS - 1)
    out = here - (STEP_SIZE * TV_WEIGHT) * tv
    for y in range(2):
        for t in range(4):
            base[0, y : y + 1, t * LANES : (t + 1) * LANES] = out[y * 4 + t : y * 4 + t + 1]


def backward_kernel(table, got, held, grad, wins):
    lane = lane_iota((8, LANES))
    places = [table[0, k] for k in range(K_MAX)]
    for k in range(K_MAX):
        block = (places[k] >> 11) & 15
        for q in range(4):
            strip = got[4 * block + q, :, k * LANES : (k + 1) * LANES]
            wins[k, 2 * q : 2 * q + 2, :] = strip.astype(jnp.float32)
    windows = []
    for k in range(K_MAX):
        low = places[k] & (WIN - 1)
        tile = wins[k]
        tile = jnp.where(
            (lane & (WIN - 1)) < WIN - low,
            pltpu.roll(tile, lax.rem(LANES - low, LANES), 1),
            pltpu.roll(tile, WIN - low, 1),
        )
        windows.append(jnp.where(places[k] >= LIVE, tile, 0.0))
    vectors = [
        jnp.concatenate([windows[k][i : i + 1, :] for i in range(8)], axis=1).astype(jnp.bfloat16)
        for k in range(ON_MATRIX)
    ]
    for j in range(8):
        rows = slice(j * LANES, (j + 1) * LANES)
        total = jnp.zeros((1, LANES), jnp.float32)
        for k in range(ON_MATRIX):
            total = total + lax.dot_general(
                vectors[k],
                held[k, rows, :],
                (((1,), (1,)), ((), ())),
                preferred_element_type=jnp.float32,
            )
        partial = jnp.zeros((LANES, LANES), jnp.float32)
        for k in range(ON_MATRIX, K_MAX):
            block = held[k, rows, :].astype(jnp.float32)
            for i in range(8):
                weight = jnp.broadcast_to(windows[k][i : i + 1, :], (LANES, LANES))
                partial = partial + block[:, i * LANES : (i + 1) * LANES] * weight
        total = total + jnp.sum(partial.T, axis=0, keepdims=True)
        y, t = j // 4, j % 4
        grad[0, y : y + 1, t * LANES : (t + 1) * LANES] = total


def smem():
    return pl.BlockSpec(memory_space=pltpu.SMEM)


def vmem():
    return pl.BlockSpec(memory_space=pltpu.VMEM)


def hbm():
    return pl.BlockSpec(memory_space=pltpu.HBM)


def in_hbm(array):
    return pltpu.with_memory_space_constraint(array, pltpu.HBM)


def on_device(image, weights, block_ids, offsets, counts, measured):
    sent, spread, held, places = pl.pallas_call(
        forward_kernel,
        out_shape=(
            jax.ShapeDtypeStruct((OWNERS, 2, WIDTH), jnp.bfloat16),
            jax.ShapeDtypeStruct((64, LANES), jnp.float32),
            jax.ShapeDtypeStruct((K_MAX, VOXELS, CELLS), jnp.bfloat16),
            jax.ShapeDtypeStruct((8, LANES), jnp.int32),
        ),
        in_specs=[hbm(), hbm(), smem(), hbm(), hbm(), hbm()],
        out_specs=(vmem(),) * 4,
        scratch_shapes=[
            pltpu.SMEM((1, 1, K_MAX), jnp.int32),
            pltpu.SMEM((1, 1, K_MAX), jnp.int32),
            pltpu.VMEM((1, 2, 512), jnp.float32),
            pltpu.VMEM((1, 4, 2048), jnp.bfloat16),
            pltpu.VMEM((2 * OWNERS, LANES), jnp.float32),
            pltpu.SemaphoreType.DMA((4,)),
            pltpu.SemaphoreType.DMA((K_MAX,)),
        ],
        compiler_params=pltpu.CompilerParams(vmem_limit_bytes=20 * MIB),
        name="forward",
    )(
        in_hbm(block_ids),
        in_hbm(offsets),
        counts,
        in_hbm(image),
        in_hbm(weights),
        in_hbm(measured),
    )
    got = lax.all_to_all(sent, VOX, 0, 0, tiled=True)
    sent, resid = pl.pallas_call(
        owner_kernel,
        out_shape=(
            jax.ShapeDtypeStruct((OWNERS, 2, WIDTH), jnp.bfloat16),
            jax.ShapeDtypeStruct((64, LANES), jnp.float32),
        ),
        in_specs=[vmem(), vmem()],
        out_specs=(vmem(), vmem()),
        scratch_shapes=[pltpu.VMEM((2 * OWNERS, WIDTH), jnp.float32)],
        compiler_params=pltpu.CompilerParams(vmem_limit_bytes=8 * MIB),
        name="owner",
    )(got, spread)
    got = lax.all_to_all(sent, VOX, 0, 0, tiled=True)
    grad = pl.pallas_call(
        backward_kernel,
        out_shape=jax.ShapeDtypeStruct((1, 2, 512), jnp.float32),
        in_specs=[vmem(), vmem(), vmem()],
        out_specs=vmem(),
        scratch_shapes=[pltpu.VMEM((K_MAX, 8, LANES), jnp.float32)],
        compiler_params=pltpu.CompilerParams(vmem_limit_bytes=20 * MIB),
        name="backward",
    )(places, got, held)
    grad = grad + lax.ppermute(grad, "core", [(0, 1), (1, 0)])
    other = lax.ppermute(grad, "z_hi", [(0, 1), (1, 0)])
    base, residual = pl.pallas_call(
        smooth_kernel,
        out_shape=(
            jax.ShapeDtypeStruct((1, 2, 512), jnp.float32),
            jax.ShapeDtypeStruct((1, 4, 2048), jnp.float32),
        ),
        in_specs=[vmem(), vmem(), vmem()],
        out_specs=(vmem(), vmem()),
        scratch_shapes=[pltpu.VMEM((2 * OWNERS, LANES), jnp.float32)],
        compiler_params=pltpu.CompilerParams(vmem_limit_bytes=8 * MIB),
        cost_estimate=pl.CostEstimate(flops=100000, bytes_accessed=1 << 19, transcendentals=4096),
        name="smooth",
    )(got, image, resid)
    return (base - STEP_SIZE * (grad + other), residual)


def solution(mesh):
    fine = Mesh(mesh.devices.reshape(4, 4, 4, 2, 2), VOX + SEN)
    placed = (
        P(VOX, None, None),
        P(VOX, SEN, None, None, None),
        P(VOX, SEN, None),
        P(VOX, SEN, None),
        P(VOX, SEN),
        P(SEN, VOX, None),
    )
    return jax.shard_map(
        on_device,
        mesh=fine,
        in_specs=placed,
        out_specs=(P(VOX, None, None), P(SEN, VOX, None)),
        check_vma=False,
    )
```

```python
import functools

import jax
import jax.numpy as jnp
from jax import lax
from jax.experimental import pallas as pl
from jax.experimental.pallas import tpu as pltpu
from jax.sharding import Mesh
from jax.sharding import PartitionSpec as P

SB = 16
WIN = 64
K_MAX = 5
VOXELS = 1024
CELLS = SB * WIN
LANES = 128
TILES = K_MAX + 1
WIDTH = TILES * LANES
OWNERS = 64
ON_MATRIX = 2
AHEAD = 2
PLACE = 2048
LIVE = 16 * PLACE
STEP_SIZE = 0.25
TV_WEIGHT = 0.3
TV_EPS = 0.01
NOWHERE = 255.0
MIB = 1 << 20

VOX = ("y", "x", "z_lo")
SEN = ("z_hi", "core")


def lane_iota(shape):
    return lax.broadcasted_iota(jnp.int32, shape, len(shape) - 1)


def as_tile(image):
    rows = [image[0, y : y + 1, t * LANES : (t + 1) * LANES] for y in range(2) for t in range(4)]
    return jnp.concatenate(rows, axis=0)


def split_three(x):
    parts = []
    for _ in range(3):
        part = x.astype(jnp.bfloat16).astype(jnp.float32)
        parts.append(part)
        x = x - part
    return parts


def forward_kernel(
    ids_hbm,
    starts_hbm,
    counts,
    image_hbm,
    weights,
    measured_hbm,
    sent,
    spread,
    held,
    places,
    ids,
    starts,
    image,
    measured,
    halo,
    small_sems,
    sems,
):
    small = []
    for i, (src, dst) in enumerate(
        (
            (image_hbm, image),
            (ids_hbm, ids),
            (starts_hbm, starts),
            (measured_hbm, measured),
        )
    ):
        small.append(pltpu.make_async_copy(src, dst, small_sems.at[i]))
        small[-1].start()
    copies = [
        pltpu.make_async_copy(weights.at[0, 0, k], held.at[k], sems.at[k]) for k in range(K_MAX)
    ]
    for k in range(K_MAX):
        copies[k].start(priority=0 if k < AHEAD else 1)
    for copy in small:
        copy.wait()

    own = measured[0].astype(jnp.float32)
    for r in range(4):
        for h in range(16):
            spread[r * 16 + h : r * 16 + h + 1, :] = own[r : r + 1, h * LANES : (h + 1) * LANES]

    plane = as_tile(image)
    turned = jnp.concatenate(split_three(plane) + [jnp.zeros((104, LANES), jnp.float32)], axis=0).T
    halo[...] = pltpu.roll(turned, 32, 1)

    voxels = jnp.concatenate([image[0, 0:1, :], image[0, 1:2, :]], axis=1).astype(jnp.bfloat16)
    lane2 = lane_iota((2, LANES))
    base = jnp.full((2, LANES), NOWHERE, jnp.float32)
    code_row = base
    block_row = jnp.full((2, LANES), -1, jnp.int32)
    live = counts[0, 0]
    table = jnp.zeros((8, LANES), jnp.int32)
    for k in range(K_MAX):
        start = starts[0, 0, k]
        place = start + ids[0, 0, k] * PLACE + jnp.where(k < live, LIVE, 0)
        table = jnp.where(lane_iota((8, LANES)) == k, place, table)
        coarse = start // WIN
        low = start - coarse * WIN
        code = (coarse & 1) * 16 + (coarse >> 1)
        block = jnp.where(k < live, ids[0, 0, k], -1)
        base = jnp.where(lane2 == 8 + k, low.astype(jnp.float32), base)
        code_row = jnp.where(lane2 == k, code.astype(jnp.float32), code_row)
        block_row = jnp.where(lane2 == k, block, block_row)
    places[...] = table
    for b in range(16):
        marked = jnp.where(block_row == b, code_row, base)
        for d in range(4 * b, 4 * b + 4):
            own_halo = halo[pl.ds(d, 2, stride=OWNERS), :]
            sent[d, :, K_MAX * LANES :] = jnp.where(lane2 < 32, marked, own_halo)

    lane = lane_iota((8, LANES))
    for k in range(K_MAX):
        copies[k].wait()
        piece = jnp.dot(voxels, held[k], preferred_element_type=jnp.float32)
        tile = jnp.concatenate([piece[:, i * LANES : (i + 1) * LANES] for i in range(8)], axis=0)
        low = lax.rem(starts[0, 0, k], WIN)
        tile = jnp.where(
            (lane & (WIN - 1)) >= low, pltpu.roll(tile, low, 1), pltpu.roll(tile, low + WIN, 1)
        )
        for q in range(4):
            strip = tile[2 * q : 2 * q + 2, :]
            for b in range(16):
                sent[4 * b + q, :, k * LANES : (k + 1) * LANES] = strip


def derivative(x):
    row = lax.broadcasted_iota(jnp.int32, x.shape, 0) & 15
    lane = lane_iota(x.shape)

    def ahead(t):
        rolled = pltpu.roll(x, LANES - t, 1)
        after = jnp.where(row == 15, 0.0, pltpu.roll(rolled, x.shape[0] - 1, 0))
        return jnp.where(lane >= LANES - t, after, rolled)

    def behind(t):
        rolled = pltpu.roll(x, t, 1)
        before = jnp.where(row == 0, 0.0, pltpu.roll(rolled, 1, 0))
        return jnp.where(lane < t, before, rolled)

    return ((behind(2) - ahead(2)) + 8.0 * (ahead(1) - behind(1))) * (1.0 / 12.0)


def owner_kernel(got, spread, sent, resid, wide):
    for d in range(OWNERS):
        wide[2 * d : 2 * d + 2, :] = got[d]
    lane = lane_iota((LANES, LANES))
    parity = lax.broadcasted_iota(jnp.int32, (LANES, LANES), 0) & 1
    within = (lane & (WIN - 1)).astype(jnp.float32)
    own_half = (lane >> 6) == parity
    first_half = (lane & 32) == 0
    slot = jnp.where(own_half, lane & 31, -1).astype(jnp.float32)
    info = wide[:, K_MAX * LANES :]
    places, strips, later = [], [], []
    for k in range(K_MAX):
        code = jnp.broadcast_to(info[:, k : k + 1], (LANES, LANES))
        low = jnp.broadcast_to(info[:, 8 + k : 9 + k], (LANES, LANES))
        following = jnp.where(code >= 16.0, code - 15.0, code + 16.0)
        wanted = jnp.where(first_half, code, following)
        places.append(jnp.where(wanted == slot, 1.0, 0.0))
        first = within >= low
        later.append(first)
        strip = wide[:, k * LANES : (k + 1) * LANES]
        strips.append(
            jnp.concatenate([jnp.where(first, strip, 0.0), jnp.where(first, 0.0, strip)], axis=1)
        )
    place = jnp.concatenate(places, axis=0).astype(jnp.bfloat16)
    strip = jnp.concatenate(split_three(jnp.concatenate(strips, axis=0)), axis=1)
    parts = lax.dot_general(
        place,
        strip.astype(jnp.bfloat16),
        (((0,), (0,)), ((), ())),
        preferred_element_type=jnp.float32,
    )
    both = parts[:, :256] + (parts[:, 256:512] + parts[:, 512:])
    lane16 = lane_iota((16, LANES)) < WIN
    rows = []
    for u in range(2):
        summed = both[64 * u : 64 * u + 32, :LANES] + both[64 * u + 32 : 64 * u + 64, LANES:]
        even = summed[0:16]
        odd = summed[16:32]
        rows.append(jnp.where(lane16, even, pltpu.roll(odd, WIN, 1)))
        rows.append(jnp.where(lane16, pltpu.roll(even, WIN, 1), odd))
    signals = jnp.concatenate(rows, axis=0)
    difference = derivative(signals) - spread[...]
    resid[...] = difference
    adjoint = -derivative(difference)
    zero = jnp.zeros((32, LANES), jnp.float32)
    table = []
    for u in range(2):
        a = adjoint[32 * u : 32 * u + 16]
        b = adjoint[32 * u + 16 : 32 * u + 32]
        half = jnp.concatenate(
            [
                jnp.where(lane16, a, pltpu.roll(b, WIN, 1)),
                jnp.where(lane16, pltpu.roll(a, WIN, 1), b),
            ],
            axis=0,
        )
        table.append(jnp.concatenate([half, zero], axis=1))
        table.append(jnp.concatenate([zero, half], axis=1))
    table = jnp.concatenate(table, axis=0).astype(jnp.bfloat16)
    cut = jnp.dot(place, table, preferred_element_type=jnp.float32)
    for k in range(K_MAX):
        mine = cut[k * LANES : (k + 1) * LANES]
        wide[:, k * LANES : (k + 1) * LANES] = jnp.where(
            later[k], mine[:, :LANES], mine[:, LANES:]
        )
    wide[:, K_MAX * LANES :] = jnp.where(
        lane < WIN,
        pltpu.roll(info, 2, 0),
        pltpu.roll(pltpu.roll(info, LANES - 2, 0), 32, 1),
    )
    for d in range(OWNERS):
        sent[d] = wide[2 * d : 2 * d + 2, :].astype(jnp.bfloat16)


def total_variation(image, before, after, is_first, is_last):
    lane = lane_iota((8, LANES))
    row = lax.broadcasted_iota(jnp.int32, (8, LANES), 0)
    last_x = (lane == LANES - 1) & ((row & 3) == 3)
    first_x = (lane == 0) & ((row & 3) == 0)

    def units(here, ahead, no_step):
        step_z = jnp.where(no_step, 0.0, ahead - here)
        step_y = jnp.where(row >= 4, 0.0, pltpu.roll(here, 4, 0) - here)
        moved = pltpu.roll(here, LANES - 1, 1)
        moved = jnp.where(lane == LANES - 1, pltpu.roll(moved, 7, 0), moved)
        step_x = jnp.where(last_x, 0.0, moved - here)
        magnitude = jnp.sqrt(step_z * step_z + step_y * step_y + step_x * step_x + TV_EPS)
        return step_z / magnitude, step_y / magnitude, step_x / magnitude

    unit_z, unit_y, unit_x = units(image, after, is_last)
    below_z, _, _ = units(before, image, is_first)
    result = below_z - unit_z
    result = result + (jnp.where(row < 4, 0.0, pltpu.roll(unit_y, 4, 0)) - unit_y)
    moved = pltpu.roll(unit_x, 1, 1)
    moved = jnp.where(lane == 0, pltpu.roll(moved, 1, 0), moved)
    return result + (jnp.where(first_x, 0.0, moved) - unit_x)


def smooth_kernel(got, image, resid, base, residual, wide):
    for r in range(4):
        for h in range(16):
            residual[0, r : r + 1, h * LANES : (h + 1) * LANES] = resid[
                r * 16 + h : r * 16 + h + 1, :
            ]
    vox = lax.axis_index(VOX)
    for d in range(OWNERS):
        wide[2 * d : 2 * d + 2, :] = got[d, :, K_MAX * LANES :].astype(jnp.float32)
    shard = jnp.concatenate([wide[pl.ds(u, OWNERS, stride=2), :] for u in range(2)], axis=0)
    whole = shard + (pltpu.roll(shard, LANES - 8, 1) + pltpu.roll(shard, LANES - 16, 1))
    turned = whole.T
    here = as_tile(image)
    tv = total_variation(here, turned[32:40], turned[64:72], vox == 0, vox == OWNERS - 1)
    out = here - (STEP_SIZE * TV_WEIGHT) * tv
    for y in range(2):
        for t in range(4):
            base[0, y : y + 1, t * LANES : (t + 1) * LANES] = out[y * 4 + t : y * 4 + t + 1]


def backward_kernel(table, got, held, grad, wins):
    lane = lane_iota((8, LANES))
    places = [table[0, k] for k in range(K_MAX)]
    for k in range(K_MAX):
        block = (places[k] >> 11) & 15
        for q in range(4):
            strip = got[4 * block + q, :, k * LANES : (k + 1) * LANES]
            wins[k, 2 * q : 2 * q + 2, :] = strip.astype(jnp.float32)
    windows = []
    for k in range(K_MAX):
        low = places[k] & (WIN - 1)
        tile = wins[k]
        tile = jnp.where(
            (lane & (WIN - 1)) < WIN - low,
            pltpu.roll(tile, lax.rem(LANES - low, LANES), 1),
            pltpu.roll(tile, WIN - low, 1),
        )
        windows.append(jnp.where(places[k] >= LIVE, tile, 0.0))
    vectors = [
        jnp.concatenate([windows[k][i : i + 1, :] for i in range(8)], axis=1).astype(jnp.bfloat16)
        for k in range(ON_MATRIX)
    ]
    for j in range(8):
        rows = slice(j * LANES, (j + 1) * LANES)
        total = jnp.zeros((1, LANES), jnp.float32)
        for k in range(ON_MATRIX):
            total = total + lax.dot_general(
                vectors[k],
                held[k, rows, :],
                (((1,), (1,)), ((), ())),
                preferred_element_type=jnp.float32,
            )
        partial = jnp.zeros((LANES, LANES), jnp.float32)
        for k in range(ON_MATRIX, K_MAX):
            block = held[k, rows, :].astype(jnp.float32)
            for i in range(8):
                weight = jnp.broadcast_to(windows[k][i : i + 1, :], (LANES, LANES))
                partial = partial + block[:, i * LANES : (i + 1) * LANES] * weight
        total = total + jnp.sum(partial.T, axis=0, keepdims=True)
        y, t = j // 4, j % 4
        grad[0, y : y + 1, t * LANES : (t + 1) * LANES] = total


def smem():
    return pl.BlockSpec(memory_space=pltpu.SMEM)


def vmem():
    return pl.BlockSpec(memory_space=pltpu.VMEM)


def hbm():
    return pl.BlockSpec(memory_space=pltpu.HBM)


def in_hbm(array):
    return pltpu.with_memory_space_constraint(array, pltpu.HBM)


def on_device(image, weights, block_ids, offsets, counts, measured):
    sent, spread, held, places = pl.pallas_call(
        forward_kernel,
        out_shape=(
            jax.ShapeDtypeStruct((OWNERS, 2, WIDTH), jnp.float32),
            jax.ShapeDtypeStruct((64, LANES), jnp.float32),
            jax.ShapeDtypeStruct((K_MAX, VOXELS, CELLS), jnp.bfloat16),
            jax.ShapeDtypeStruct((8, LANES), jnp.int32),
        ),
        in_specs=[hbm(), hbm(), smem(), hbm(), hbm(), hbm()],
        out_specs=(vmem(),) * 4,
        scratch_shapes=[
            pltpu.SMEM((1, 1, K_MAX), jnp.int32),
            pltpu.SMEM((1, 1, K_MAX), jnp.int32),
            pltpu.VMEM((1, 2, 512), jnp.float32),
            pltpu.VMEM((1, 4, 2048), jnp.bfloat16),
            pltpu.VMEM((2 * OWNERS, LANES), jnp.float32),
            pltpu.SemaphoreType.DMA((4,)),
            pltpu.SemaphoreType.DMA((K_MAX,)),
        ],
        compiler_params=pltpu.CompilerParams(vmem_limit_bytes=20 * MIB),
        name="forward",
    )(
        in_hbm(block_ids),
        in_hbm(offsets),
        counts,
        in_hbm(image),
        in_hbm(weights),
        in_hbm(measured),
    )
    got = lax.all_to_all(sent, VOX, 0, 0, tiled=True)
    sent, resid = pl.pallas_call(
        owner_kernel,
        out_shape=(
            jax.ShapeDtypeStruct((OWNERS, 2, WIDTH), jnp.bfloat16),
            jax.ShapeDtypeStruct((64, LANES), jnp.float32),
        ),
        in_specs=[vmem(), vmem()],
        out_specs=(vmem(), vmem()),
        scratch_shapes=[pltpu.VMEM((2 * OWNERS, WIDTH), jnp.float32)],
        compiler_params=pltpu.CompilerParams(vmem_limit_bytes=8 * MIB),
        name="owner",
    )(got, spread)
    got = lax.all_to_all(sent, VOX, 0, 0, tiled=True)
    grad = pl.pallas_call(
        backward_kernel,
        out_shape=jax.ShapeDtypeStruct((1, 2, 512), jnp.float32),
        in_specs=[vmem(), vmem(), vmem()],
        out_specs=vmem(),
        scratch_shapes=[pltpu.VMEM((K_MAX, 8, LANES), jnp.float32)],
        compiler_params=pltpu.CompilerParams(vmem_limit_bytes=20 * MIB),
        name="backward",
    )(places, got, held)
    grad = grad + lax.ppermute(grad, "core", [(0, 1), (1, 0)])
    other = lax.ppermute(grad, "z_hi", [(0, 1), (1, 0)])
    base, residual = pl.pallas_call(
        smooth_kernel,
        out_shape=(
            jax.ShapeDtypeStruct((1, 2, 512), jnp.float32),
            jax.ShapeDtypeStruct((1, 4, 2048), jnp.float32),
        ),
        in_specs=[vmem(), vmem(), vmem()],
        out_specs=(vmem(), vmem()),
        scratch_shapes=[pltpu.VMEM((2 * OWNERS, LANES), jnp.float32)],
        compiler_params=pltpu.CompilerParams(vmem_limit_bytes=8 * MIB),
        cost_estimate=pl.CostEstimate(flops=100000, bytes_accessed=1 << 19, transcendentals=4096),
        name="smooth",
    )(got, image, resid)
    return (base - STEP_SIZE * (grad + other), residual)


def solution(mesh):
    fine = Mesh(mesh.devices.reshape(4, 4, 4, 2, 2), VOX + SEN)
    placed = (
        P(VOX, None, None),
        P(VOX, SEN, None, None, None),
        P(VOX, SEN, None),
        P(VOX, SEN, None),
        P(VOX, SEN),
        P(SEN, VOX, None),
    )
    return jax.shard_map(
        on_device,
        mesh=fine,
        in_specs=placed,
        out_specs=(P(VOX, None, None), P(SEN, VOX, None)),
        check_vma=False,
    )
```

```python
import functools

import jax
import jax.numpy as jnp
from jax import lax
from jax.experimental import pallas as pl
from jax.experimental.pallas import tpu as pltpu
from jax.sharding import Mesh
from jax.sharding import PartitionSpec as P

SB = 16
WIN = 64
K_MAX = 5
VOXELS = 1024
CELLS = SB * WIN
LANES = 128
TILES = K_MAX + 1
WIDTH = TILES * LANES
OWNERS = 64
ON_MATRIX = 2
AHEAD = 2
PLACE = 2048
LIVE = 16 * PLACE
STEP_SIZE = 0.25
TV_WEIGHT = 0.3
TV_EPS = 0.01
NOWHERE = 255.0
MIB = 1 << 20

VOX = ("y", "x", "z_lo")
SEN = ("z_hi", "core")


def lane_iota(shape):
    return lax.broadcasted_iota(jnp.int32, shape, len(shape) - 1)


def as_tile(image):
    rows = [image[0, y : y + 1, t * LANES : (t + 1) * LANES] for y in range(2) for t in range(4)]
    return jnp.concatenate(rows, axis=0)


def split_three(x):
    parts = []
    for _ in range(3):
        part = x.astype(jnp.bfloat16).astype(jnp.float32)
        parts.append(part)
        x = x - part
    return parts


def forward_kernel(
    ids_hbm,
    starts_hbm,
    counts,
    image_hbm,
    weights,
    measured_hbm,
    sent,
    spread,
    held,
    places,
    ids,
    starts,
    image,
    measured,
    halo,
    small_sems,
    sems,
):
    small = []
    for i, (src, dst) in enumerate(
        (
            (image_hbm, image),
            (ids_hbm, ids),
            (starts_hbm, starts),
            (measured_hbm, measured),
        )
    ):
        small.append(pltpu.make_async_copy(src, dst, small_sems.at[i]))
        small[-1].start()
    copies = [
        pltpu.make_async_copy(weights.at[0, 0, k], held.at[k], sems.at[k]) for k in range(K_MAX)
    ]
    for k in range(K_MAX):
        copies[k].start(priority=0 if k < AHEAD else 1)
    for copy in small:
        copy.wait()

    own = measured[0].astype(jnp.float32)
    for r in range(4):
        for h in range(16):
            spread[r * 16 + h : r * 16 + h + 1, :] = own[r : r + 1, h * LANES : (h + 1) * LANES]

    plane = as_tile(image)
    turned = jnp.concatenate(split_three(plane) + [jnp.zeros((104, LANES), jnp.float32)], axis=0).T
    halo[...] = pltpu.roll(turned, 32, 1)

    voxels = jnp.concatenate([image[0, 0:1, :], image[0, 1:2, :]], axis=1).astype(jnp.bfloat16)
    lane2 = lane_iota((2, LANES))
    base = jnp.full((2, LANES), NOWHERE, jnp.float32)
    code_row = base
    block_row = jnp.full((2, LANES), -1, jnp.int32)
    live = counts[0, 0]
    table = jnp.zeros((8, LANES), jnp.int32)
    for k in range(K_MAX):
        start = starts[0, 0, k]
        place = start + ids[0, 0, k] * PLACE + jnp.where(k < live, LIVE, 0)
        table = jnp.where(lane_iota((8, LANES)) == k, place, table)
        coarse = start // WIN
        low = start - coarse * WIN
        code = (coarse & 1) * 16 + (coarse >> 1)
        block = jnp.where(k < live, ids[0, 0, k], -1)
        base = jnp.where(lane2 == 8 + k, low.astype(jnp.float32), base)
        code_row = jnp.where(lane2 == k, code.astype(jnp.float32), code_row)
        block_row = jnp.where(lane2 == k, block, block_row)
    places[...] = table
    for b in range(16):
        marked = jnp.where(block_row == b, code_row, base)
        for d in range(4 * b, 4 * b + 4):
            own_halo = halo[pl.ds(d, 2, stride=OWNERS), :]
            sent[d, :, K_MAX * LANES :] = jnp.where(lane2 < 32, marked, own_halo).astype(
                jnp.bfloat16
            )

    lane = lane_iota((8, LANES))
    for k in range(K_MAX):
        copies[k].wait()
        piece = jnp.dot(voxels, held[k], preferred_element_type=jnp.float32)
        tile = jnp.concatenate([piece[:, i * LANES : (i + 1) * LANES] for i in range(8)], axis=0)
        low = lax.rem(starts[0, 0, k], WIN)
        tile = jnp.where(
            (lane & (WIN - 1)) >= low, pltpu.roll(tile, low, 1), pltpu.roll(tile, low + WIN, 1)
        )
        for q in range(4):
            strip = tile[2 * q : 2 * q + 2, :].astype(jnp.bfloat16)
            for b in range(16):
                sent[4 * b + q, :, k * LANES : (k + 1) * LANES] = strip


def derivative(x):
    row = lax.broadcasted_iota(jnp.int32, x.shape, 0) & 15
    lane = lane_iota(x.shape)

    def ahead(t):
        rolled = pltpu.roll(x, LANES - t, 1)
        after = jnp.where(row == 15, 0.0, pltpu.roll(rolled, x.shape[0] - 1, 0))
        return jnp.where(lane >= LANES - t, after, rolled)

    def behind(t):
        rolled = pltpu.roll(x, t, 1)
        before = jnp.where(row == 0, 0.0, pltpu.roll(rolled, 1, 0))
        return jnp.where(lane < t, before, rolled)

    return ((behind(2) - ahead(2)) + 8.0 * (ahead(1) - behind(1))) * (1.0 / 12.0)


def owner_kernel(got, spread, sent, resid, wide):
    wide[...] = got[...].reshape(2 * OWNERS, WIDTH).astype(jnp.float32)
    lane = lane_iota((LANES, LANES))
    parity = lax.broadcasted_iota(jnp.int32, (LANES, LANES), 0) & 1
    within = (lane & (WIN - 1)).astype(jnp.float32)
    own_half = (lane >> 6) == parity
    first_half = (lane & 32) == 0
    slot = jnp.where(own_half, lane & 31, -1).astype(jnp.float32)
    info = wide[:, K_MAX * LANES :]
    shape = (LANES, 2 * K_MAX * LANES)
    source = lax.broadcasted_iota(jnp.int32, shape, 1) >> 7
    source = jnp.where(source < K_MAX, source, source + 8 - K_MAX)
    pick = jnp.where(lax.broadcasted_iota(jnp.int32, shape, 0) == source, 1.0, 0.0)
    spread_out = jnp.dot(
        jnp.where(lane < 16, info, 0.0).astype(jnp.bfloat16),
        pick.astype(jnp.bfloat16),
        preferred_element_type=jnp.float32,
    )
    places, strips, later = [], [], []
    for k in range(K_MAX):
        code = spread_out[:, k * LANES : (k + 1) * LANES]
        low = spread_out[:, (K_MAX + k) * LANES : (K_MAX + k + 1) * LANES]
        following = jnp.where(code >= 16.0, code - 15.0, code + 16.0)
        wanted = jnp.where(first_half, code, following)
        places.append(jnp.where(wanted == slot, 1.0, 0.0))
        first = within >= low
        later.append(first)
        strip = wide[:, k * LANES : (k + 1) * LANES]
        strips.append(
            jnp.concatenate([jnp.where(first, strip, 0.0), jnp.where(first, 0.0, strip)], axis=1)
        )
    place = jnp.concatenate(places, axis=0).astype(jnp.bfloat16)
    strip = jnp.concatenate(strips, axis=0).astype(jnp.bfloat16)
    both = lax.dot_general(
        place, strip, (((0,), (0,)), ((), ())), preferred_element_type=jnp.float32
    )
    lane16 = lane_iota((16, LANES)) < WIN
    rows = []
    for u in range(2):
        summed = both[64 * u : 64 * u + 32, :LANES] + both[64 * u + 32 : 64 * u + 64, LANES:]
        even = summed[0:16]
        odd = summed[16:32]
        rows.append(jnp.where(lane16, even, pltpu.roll(odd, WIN, 1)))
        rows.append(jnp.where(lane16, pltpu.roll(even, WIN, 1), odd))
    signals = jnp.concatenate(rows, axis=0)
    difference = derivative(signals) - spread[...]
    resid[...] = difference
    adjoint = -derivative(difference)
    zero = jnp.zeros((32, LANES), jnp.float32)
    table = []
    for u in range(2):
        a = adjoint[32 * u : 32 * u + 16]
        b = adjoint[32 * u + 16 : 32 * u + 32]
        half = jnp.concatenate(
            [
                jnp.where(lane16, a, pltpu.roll(b, WIN, 1)),
                jnp.where(lane16, pltpu.roll(a, WIN, 1), b),
            ],
            axis=0,
        )
        table.append(jnp.concatenate([half, zero], axis=1))
        table.append(jnp.concatenate([zero, half], axis=1))
    table = jnp.concatenate(table, axis=0).astype(jnp.bfloat16)
    cut = jnp.dot(place, table, preferred_element_type=jnp.float32)
    for k in range(K_MAX):
        mine = cut[k * LANES : (k + 1) * LANES]
        wide[:, k * LANES : (k + 1) * LANES] = jnp.where(
            later[k], mine[:, :LANES], mine[:, LANES:]
        )
    wide[:, K_MAX * LANES :] = jnp.where(
        lane < WIN,
        pltpu.roll(info, 2, 0),
        pltpu.roll(pltpu.roll(info, LANES - 2, 0), 32, 1),
    )
    sent[...] = wide[...].astype(jnp.bfloat16).reshape(OWNERS, 2, WIDTH)


def total_variation(image, before, after, is_first, is_last):
    lane = lane_iota((8, LANES))
    row = lax.broadcasted_iota(jnp.int32, (8, LANES), 0)
    last_x = (lane == LANES - 1) & ((row & 3) == 3)
    first_x = (lane == 0) & ((row & 3) == 0)

    def units(here, ahead, no_step):
        step_z = jnp.where(no_step, 0.0, ahead - here)
        step_y = jnp.where(row >= 4, 0.0, pltpu.roll(here, 4, 0) - here)
        moved = pltpu.roll(here, LANES - 1, 1)
        moved = jnp.where(lane == LANES - 1, pltpu.roll(moved, 7, 0), moved)
        step_x = jnp.where(last_x, 0.0, moved - here)
        magnitude = jnp.sqrt(step_z * step_z + step_y * step_y + step_x * step_x + TV_EPS)
        return step_z / magnitude, step_y / magnitude, step_x / magnitude

    unit_z, unit_y, unit_x = units(image, after, is_last)
    below_z, _, _ = units(before, image, is_first)
    result = below_z - unit_z
    result = result + (jnp.where(row < 4, 0.0, pltpu.roll(unit_y, 4, 0)) - unit_y)
    moved = pltpu.roll(unit_x, 1, 1)
    moved = jnp.where(lane == 0, pltpu.roll(moved, 1, 0), moved)
    return result + (jnp.where(first_x, 0.0, moved) - unit_x)


def smooth_kernel(got, image, resid, base, residual, wide):
    for r in range(4):
        for h in range(16):
            residual[0, r : r + 1, h * LANES : (h + 1) * LANES] = resid[
                r * 16 + h : r * 16 + h + 1, :
            ]
    vox = lax.axis_index(VOX)
    for d in range(OWNERS):
        wide[2 * d : 2 * d + 2, :] = got[d, :, K_MAX * LANES :].astype(jnp.float32)
    shard = jnp.concatenate([wide[pl.ds(u, OWNERS, stride=2), :] for u in range(2)], axis=0)
    whole = shard + (pltpu.roll(shard, LANES - 8, 1) + pltpu.roll(shard, LANES - 16, 1))
    turned = whole.T
    here = as_tile(image)
    tv = total_variation(here, turned[32:40], turned[64:72], vox == 0, vox == OWNERS - 1)
    out = here - (STEP_SIZE * TV_WEIGHT) * tv
    for y in range(2):
        for t in range(4):
            base[0, y : y + 1, t * LANES : (t + 1) * LANES] = out[y * 4 + t : y * 4 + t + 1]


def backward_kernel(table, got, held, grad, wins):
    lane = lane_iota((8, LANES))
    places = [table[0, k] for k in range(K_MAX)]
    for k in range(K_MAX):
        block = (places[k] >> 11) & 15
        for q in range(4):
            strip = got[4 * block + q, :, k * LANES : (k + 1) * LANES]
            wins[k, 2 * q : 2 * q + 2, :] = strip.astype(jnp.float32)
    windows = []
    for k in range(K_MAX):
        low = places[k] & (WIN - 1)
        tile = wins[k]
        tile = jnp.where(
            (lane & (WIN - 1)) < WIN - low,
            pltpu.roll(tile, lax.rem(LANES - low, LANES), 1),
            pltpu.roll(tile, WIN - low, 1),
        )
        windows.append(jnp.where(places[k] >= LIVE, tile, 0.0))
    vectors = [
        jnp.concatenate([windows[k][i : i + 1, :] for i in range(8)], axis=1).astype(jnp.bfloat16)
        for k in range(ON_MATRIX)
    ]
    for j in range(8):
        rows = slice(j * LANES, (j + 1) * LANES)
        total = jnp.zeros((1, LANES), jnp.float32)
        for k in range(ON_MATRIX):
            total = total + lax.dot_general(
                vectors[k],
                held[k, rows, :],
                (((1,), (1,)), ((), ())),
                preferred_element_type=jnp.float32,
            )
        partial = jnp.zeros((LANES, LANES), jnp.float32)
        for k in range(ON_MATRIX, K_MAX):
            block = held[k, rows, :].astype(jnp.float32)
            for i in range(8):
                weight = jnp.broadcast_to(windows[k][i : i + 1, :], (LANES, LANES))
                partial = partial + block[:, i * LANES : (i + 1) * LANES] * weight
        total = total + jnp.sum(partial.T, axis=0, keepdims=True)
        y, t = j // 4, j % 4
        grad[0, y : y + 1, t * LANES : (t + 1) * LANES] = total


def smem():
    return pl.BlockSpec(memory_space=pltpu.SMEM)


def vmem():
    return pl.BlockSpec(memory_space=pltpu.VMEM)


def hbm():
    return pl.BlockSpec(memory_space=pltpu.HBM)


def in_hbm(array):
    return pltpu.with_memory_space_constraint(array, pltpu.HBM)


def on_device(image, weights, block_ids, offsets, counts, measured):
    sent, spread, held, places = pl.pallas_call(
        forward_kernel,
        out_shape=(
            jax.ShapeDtypeStruct((OWNERS, 2, WIDTH), jnp.bfloat16),
            jax.ShapeDtypeStruct((64, LANES), jnp.float32),
            jax.ShapeDtypeStruct((K_MAX, VOXELS, CELLS), jnp.bfloat16),
            jax.ShapeDtypeStruct((8, LANES), jnp.int32),
        ),
        in_specs=[hbm(), hbm(), smem(), hbm(), hbm(), hbm()],
        out_specs=(vmem(),) * 4,
        scratch_shapes=[
            pltpu.SMEM((1, 1, K_MAX), jnp.int32),
            pltpu.SMEM((1, 1, K_MAX), jnp.int32),
            pltpu.VMEM((1, 2, 512), jnp.float32),
            pltpu.VMEM((1, 4, 2048), jnp.bfloat16),
            pltpu.VMEM((2 * OWNERS, LANES), jnp.float32),
            pltpu.SemaphoreType.DMA((4,)),
            pltpu.SemaphoreType.DMA((K_MAX,)),
        ],
        compiler_params=pltpu.CompilerParams(vmem_limit_bytes=20 * MIB),
        name="forward",
    )(
        in_hbm(block_ids),
        in_hbm(offsets),
        counts,
        in_hbm(image),
        in_hbm(weights),
        in_hbm(measured),
    )
    got = lax.all_to_all(sent, VOX, 0, 0, tiled=True)
    sent, resid = pl.pallas_call(
        owner_kernel,
        out_shape=(
            jax.ShapeDtypeStruct((OWNERS, 2, WIDTH), jnp.bfloat16),
            jax.ShapeDtypeStruct((64, LANES), jnp.float32),
        ),
        in_specs=[vmem(), vmem()],
        out_specs=(vmem(), vmem()),
        scratch_shapes=[pltpu.VMEM((2 * OWNERS, WIDTH), jnp.float32)],
        compiler_params=pltpu.CompilerParams(vmem_limit_bytes=8 * MIB),
        name="owner",
    )(got, spread)
    got = lax.all_to_all(sent, VOX, 0, 0, tiled=True)
    grad = pl.pallas_call(
        backward_kernel,
        out_shape=jax.ShapeDtypeStruct((1, 2, 512), jnp.float32),
        in_specs=[vmem(), vmem(), vmem()],
        out_specs=vmem(),
        scratch_shapes=[pltpu.VMEM((K_MAX, 8, LANES), jnp.float32)],
        compiler_params=pltpu.CompilerParams(vmem_limit_bytes=20 * MIB),
        name="backward",
    )(places, got, held)
    grad = grad + lax.ppermute(grad, "z_hi", [(0, 1), (1, 0)])
    other = lax.ppermute(grad, "core", [(0, 1), (1, 0)])
    base, residual = pl.pallas_call(
        smooth_kernel,
        out_shape=(
            jax.ShapeDtypeStruct((1, 2, 512), jnp.float32),
            jax.ShapeDtypeStruct((1, 4, 2048), jnp.float32),
        ),
        in_specs=[vmem(), vmem(), vmem()],
        out_specs=(vmem(), vmem()),
        scratch_shapes=[pltpu.VMEM((2 * OWNERS, LANES), jnp.float32)],
        compiler_params=pltpu.CompilerParams(vmem_limit_bytes=8 * MIB),
        cost_estimate=pl.CostEstimate(flops=100000, bytes_accessed=1 << 19, transcendentals=4096),
        name="smooth",
    )(got, image, resid)
    return (base - STEP_SIZE * (grad + other), residual)


def solution(mesh):
    fine = Mesh(mesh.devices.reshape(4, 4, 4, 2, 2), VOX + SEN)
    placed = (
        P(VOX, None, None),
        P(VOX, SEN, None, None, None),
        P(VOX, SEN, None),
        P(VOX, SEN, None),
        P(VOX, SEN),
        P(SEN, VOX, None),
    )
    return jax.shard_map(
        on_device,
        mesh=fine,
        in_specs=placed,
        out_specs=(P(VOX, None, None), P(SEN, VOX, None)),
        check_vma=False,
    )
```

```python
import functools

import jax
import jax.numpy as jnp
from jax import lax
from jax.experimental import pallas as pl
from jax.experimental.pallas import tpu as pltpu
from jax.sharding import Mesh
from jax.sharding import PartitionSpec as P

SB = 16
WIN = 64
K_MAX = 5
VOXELS = 1024
CELLS = SB * WIN
LANES = 128
TILES = K_MAX + 1
WIDTH = TILES * LANES
OWNERS = 64
ON_MATRIX = 2
AHEAD = 2
PLACE = 2048
LIVE = 16 * PLACE
STEP_SIZE = 0.25
TV_WEIGHT = 0.3
TV_EPS = 0.01
NOWHERE = 255.0
MIB = 1 << 20

VOX = ("y", "x", "z_lo")
SEN = ("z_hi", "core")


def lane_iota(shape):
    return lax.broadcasted_iota(jnp.int32, shape, len(shape) - 1)


def as_tile(image):
    rows = [image[0, y : y + 1, t * LANES : (t + 1) * LANES] for y in range(2) for t in range(4)]
    return jnp.concatenate(rows, axis=0)


def split_three(x):
    parts = []
    for _ in range(3):
        part = x.astype(jnp.bfloat16).astype(jnp.float32)
        parts.append(part)
        x = x - part
    return parts


def forward_kernel(
    ids_hbm,
    starts_hbm,
    counts,
    image_hbm,
    weights,
    measured_hbm,
    sent,
    spread,
    held,
    places,
    ids,
    starts,
    image,
    measured,
    halo,
    small_sems,
    sems,
):
    small = []
    for i, (src, dst) in enumerate(
        (
            (image_hbm, image),
            (ids_hbm, ids),
            (starts_hbm, starts),
            (measured_hbm, measured),
        )
    ):
        small.append(pltpu.make_async_copy(src, dst, small_sems.at[i]))
        small[-1].start()
    copies = [
        pltpu.make_async_copy(weights.at[0, 0, k], held.at[k], sems.at[k]) for k in range(K_MAX)
    ]
    for k in range(K_MAX):
        copies[k].start(priority=0 if k < AHEAD else 1)
    for copy in small:
        copy.wait()

    own = measured[0].astype(jnp.float32)
    for r in range(4):
        for h in range(16):
            spread[r * 16 + h : r * 16 + h + 1, :] = own[r : r + 1, h * LANES : (h + 1) * LANES]

    plane = as_tile(image)
    turned = jnp.concatenate(split_three(plane) + [jnp.zeros((104, LANES), jnp.float32)], axis=0).T
    halo[...] = pltpu.roll(turned, 32, 1)

    voxels = jnp.concatenate([image[0, 0:1, :], image[0, 1:2, :]], axis=1).astype(jnp.bfloat16)
    lane2 = lane_iota((2, LANES))
    base = jnp.full((2, LANES), NOWHERE, jnp.float32)
    code_row = base
    block_row = jnp.full((2, LANES), -1, jnp.int32)
    live = counts[0, 0]
    table = jnp.zeros((8, LANES), jnp.int32)
    for k in range(K_MAX):
        start = starts[0, 0, k]
        place = start + ids[0, 0, k] * PLACE + jnp.where(k < live, LIVE, 0)
        table = jnp.where(lane_iota((8, LANES)) == k, place, table)
        coarse = start // WIN
        low = start - coarse * WIN
        code = (coarse & 1) * 16 + (coarse >> 1)
        block = jnp.where(k < live, ids[0, 0, k], -1)
        base = jnp.where(lane2 == 8 + k, low.astype(jnp.float32), base)
        code_row = jnp.where(lane2 == k, code.astype(jnp.float32), code_row)
        block_row = jnp.where(lane2 == k, block, block_row)
    places[...] = table
    for b in range(16):
        marked = jnp.where(block_row == b, code_row, base)
        for d in range(4 * b, 4 * b + 4):
            own_halo = halo[pl.ds(d, 2, stride=OWNERS), :]
            sent[d, :, K_MAX * LANES :] = jnp.where(lane2 < 32, marked, own_halo).astype(
                jnp.bfloat16
            )

    lane = lane_iota((8, LANES))
    for k in range(K_MAX):
        copies[k].wait()
        piece = jnp.dot(voxels, held[k], preferred_element_type=jnp.float32)
        tile = jnp.concatenate([piece[:, i * LANES : (i + 1) * LANES] for i in range(8)], axis=0)
        low = lax.rem(starts[0, 0, k], WIN)
        tile = jnp.where(
            (lane & (WIN - 1)) >= low, pltpu.roll(tile, low, 1), pltpu.roll(tile, low + WIN, 1)
        )
        for q in range(4):
            strip = tile[2 * q : 2 * q + 2, :].astype(jnp.bfloat16)
            for b in range(16):
                sent[4 * b + q, :, k * LANES : (k + 1) * LANES] = strip


def derivative(x):
    row = lax.broadcasted_iota(jnp.int32, x.shape, 0) & 15
    lane = lane_iota(x.shape)

    def ahead(t):
        rolled = pltpu.roll(x, LANES - t, 1)
        after = jnp.where(row == 15, 0.0, pltpu.roll(rolled, x.shape[0] - 1, 0))
        return jnp.where(lane >= LANES - t, after, rolled)

    def behind(t):
        rolled = pltpu.roll(x, t, 1)
        before = jnp.where(row == 0, 0.0, pltpu.roll(rolled, 1, 0))
        return jnp.where(lane < t, before, rolled)

    return ((behind(2) - ahead(2)) + 8.0 * (ahead(1) - behind(1))) * (1.0 / 12.0)


def owner_kernel(got, spread, sent, resid, wide):
    wide[...] = got[...].reshape(2 * OWNERS, WIDTH).astype(jnp.float32)
    lane = lane_iota((LANES, LANES))
    parity = lax.broadcasted_iota(jnp.int32, (LANES, LANES), 0) & 1
    within = (lane & (WIN - 1)).astype(jnp.float32)
    own_half = (lane >> 6) == parity
    first_half = (lane & 32) == 0
    slot = jnp.where(own_half, lane & 31, -1).astype(jnp.float32)
    info = wide[:, K_MAX * LANES :]
    shape = (LANES, 2 * K_MAX * LANES)
    source = lax.broadcasted_iota(jnp.int32, shape, 1) >> 7
    source = jnp.where(source < K_MAX, source, source + 8 - K_MAX)
    pick = jnp.where(lax.broadcasted_iota(jnp.int32, shape, 0) == source, 1.0, 0.0)
    spread_out = jnp.dot(
        jnp.where(lane < 16, info, 0.0).astype(jnp.bfloat16),
        pick.astype(jnp.bfloat16),
        preferred_element_type=jnp.float32,
    )
    places, strips, later = [], [], []
    for k in range(K_MAX):
        code = spread_out[:, k * LANES : (k + 1) * LANES]
        low = spread_out[:, (K_MAX + k) * LANES : (K_MAX + k + 1) * LANES]
        following = jnp.where(code >= 16.0, code - 15.0, code + 16.0)
        wanted = jnp.where(first_half, code, following)
        places.append(jnp.where(wanted == slot, 1.0, 0.0))
        first = within >= low
        later.append(first)
        strip = wide[:, k * LANES : (k + 1) * LANES]
        strips.append(
            jnp.concatenate([jnp.where(first, strip, 0.0), jnp.where(first, 0.0, strip)], axis=1)
        )
    place = jnp.concatenate(places, axis=0).astype(jnp.bfloat16)
    strip = jnp.concatenate(strips, axis=0).astype(jnp.bfloat16)
    both = lax.dot_general(
        place, strip, (((0,), (0,)), ((), ())), preferred_element_type=jnp.float32
    )
    lane16 = lane_iota((16, LANES)) < WIN
    rows = []
    for u in range(2):
        summed = both[64 * u : 64 * u + 32, :LANES] + both[64 * u + 32 : 64 * u + 64, LANES:]
        even = summed[0:16]
        odd = summed[16:32]
        rows.append(jnp.where(lane16, even, pltpu.roll(odd, WIN, 1)))
        rows.append(jnp.where(lane16, pltpu.roll(even, WIN, 1), odd))
    signals = jnp.concatenate(rows, axis=0)
    difference = derivative(signals) - spread[...]
    resid[...] = difference
    adjoint = -derivative(difference)
    zero = jnp.zeros((32, LANES), jnp.float32)
    table = []
    for u in range(2):
        a = adjoint[32 * u : 32 * u + 16]
        b = adjoint[32 * u + 16 : 32 * u + 32]
        half = jnp.concatenate(
            [
                jnp.where(lane16, a, pltpu.roll(b, WIN, 1)),
                jnp.where(lane16, pltpu.roll(a, WIN, 1), b),
            ],
            axis=0,
        )
        table.append(jnp.concatenate([half, zero], axis=1))
        table.append(jnp.concatenate([zero, half], axis=1))
    table = jnp.concatenate(table, axis=0).astype(jnp.bfloat16)
    cut = jnp.dot(place, table, preferred_element_type=jnp.float32)
    for k in range(K_MAX):
        mine = cut[k * LANES : (k + 1) * LANES]
        wide[:, k * LANES : (k + 1) * LANES] = jnp.where(
            later[k], mine[:, :LANES], mine[:, LANES:]
        )
    wide[:, K_MAX * LANES :] = jnp.where(
        lane < WIN,
        pltpu.roll(info, 2, 0),
        pltpu.roll(pltpu.roll(info, LANES - 2, 0), 32, 1),
    )
    sent[...] = wide[...].astype(jnp.bfloat16).reshape(OWNERS, 2, WIDTH)


def total_variation(image, before, after, is_first, is_last):
    lane = lane_iota((8, LANES))
    row = lax.broadcasted_iota(jnp.int32, (8, LANES), 0)
    last_x = (lane == LANES - 1) & ((row & 3) == 3)
    first_x = (lane == 0) & ((row & 3) == 0)

    def units(here, ahead, no_step):
        step_z = jnp.where(no_step, 0.0, ahead - here)
        step_y = jnp.where(row >= 4, 0.0, pltpu.roll(here, 4, 0) - here)
        moved = pltpu.roll(here, LANES - 1, 1)
        moved = jnp.where(lane == LANES - 1, pltpu.roll(moved, 7, 0), moved)
        step_x = jnp.where(last_x, 0.0, moved - here)
        magnitude = jnp.sqrt(step_z * step_z + step_y * step_y + step_x * step_x + TV_EPS)
        return step_z / magnitude, step_y / magnitude, step_x / magnitude

    unit_z, unit_y, unit_x = units(image, after, is_last)
    below_z, _, _ = units(before, image, is_first)
    result = below_z - unit_z
    result = result + (jnp.where(row < 4, 0.0, pltpu.roll(unit_y, 4, 0)) - unit_y)
    moved = pltpu.roll(unit_x, 1, 1)
    moved = jnp.where(lane == 0, pltpu.roll(moved, 1, 0), moved)
    return result + (jnp.where(first_x, 0.0, moved) - unit_x)


def smooth_kernel(got, image, resid, base, residual, wide):
    for r in range(4):
        for h in range(16):
            residual[0, r : r + 1, h * LANES : (h + 1) * LANES] = resid[
                r * 16 + h : r * 16 + h + 1, :
            ]
    vox = lax.axis_index(VOX)
    for d in range(OWNERS):
        wide[2 * d : 2 * d + 2, :] = got[d, :, K_MAX * LANES :].astype(jnp.float32)
    shard = jnp.concatenate([wide[pl.ds(u, OWNERS, stride=2), :] for u in range(2)], axis=0)
    whole = shard + (pltpu.roll(shard, LANES - 8, 1) + pltpu.roll(shard, LANES - 16, 1))
    turned = whole.T
    here = as_tile(image)
    tv = total_variation(here, turned[32:40], turned[64:72], vox == 0, vox == OWNERS - 1)
    out = here - (STEP_SIZE * TV_WEIGHT) * tv
    for y in range(2):
        for t in range(4):
            base[0, y : y + 1, t * LANES : (t + 1) * LANES] = out[y * 4 + t : y * 4 + t + 1]


def backward_kernel(table, got, held, grad, wins):
    lane = lane_iota((8, LANES))
    places = [table[0, k] for k in range(K_MAX)]
    for k in range(K_MAX):
        block = (places[k] >> 11) & 15
        for q in range(4):
            strip = got[4 * block + q, :, k * LANES : (k + 1) * LANES]
            wins[k, 2 * q : 2 * q + 2, :] = strip.astype(jnp.float32)
    windows = []
    for k in range(K_MAX):
        low = places[k] & (WIN - 1)
        tile = wins[k]
        tile = jnp.where(
            (lane & (WIN - 1)) < WIN - low,
            pltpu.roll(tile, lax.rem(LANES - low, LANES), 1),
            pltpu.roll(tile, WIN - low, 1),
        )
        windows.append(jnp.where(places[k] >= LIVE, tile, 0.0))
    vectors = [
        jnp.concatenate([windows[k][i : i + 1, :] for i in range(8)], axis=1).astype(jnp.bfloat16)
        for k in range(ON_MATRIX)
    ]
    for j in range(8):
        rows = slice(j * LANES, (j + 1) * LANES)
        total = jnp.zeros((1, LANES), jnp.float32)
        for k in range(ON_MATRIX):
            total = total + lax.dot_general(
                vectors[k],
                held[k, rows, :],
                (((1,), (1,)), ((), ())),
                preferred_element_type=jnp.float32,
            )
        partial = jnp.zeros((LANES, LANES), jnp.float32)
        for k in range(ON_MATRIX, K_MAX):
            block = held[k, rows, :].astype(jnp.float32)
            for i in range(8):
                weight = jnp.broadcast_to(windows[k][i : i + 1, :], (LANES, LANES))
                partial = partial + block[:, i * LANES : (i + 1) * LANES] * weight
        total = total + jnp.sum(partial.T, axis=0, keepdims=True)
        y, t = j // 4, j % 4
        grad[0, y : y + 1, t * LANES : (t + 1) * LANES] = total


def smem():
    return pl.BlockSpec(memory_space=pltpu.SMEM)


def vmem():
    return pl.BlockSpec(memory_space=pltpu.VMEM)


def hbm():
    return pl.BlockSpec(memory_space=pltpu.HBM)


def in_hbm(array):
    return pltpu.with_memory_space_constraint(array, pltpu.HBM)


def on_device(image, weights, block_ids, offsets, counts, measured):
    sent, spread, held, places = pl.pallas_call(
        forward_kernel,
        out_shape=(
            jax.ShapeDtypeStruct((OWNERS, 2, WIDTH), jnp.bfloat16),
            jax.ShapeDtypeStruct((64, LANES), jnp.float32),
            jax.ShapeDtypeStruct((K_MAX, VOXELS, CELLS), jnp.bfloat16),
            jax.ShapeDtypeStruct((8, LANES), jnp.int32),
        ),
        in_specs=[hbm(), hbm(), smem(), hbm(), hbm(), hbm()],
        out_specs=(vmem(),) * 4,
        scratch_shapes=[
            pltpu.SMEM((1, 1, K_MAX), jnp.int32),
            pltpu.SMEM((1, 1, K_MAX), jnp.int32),
            pltpu.VMEM((1, 2, 512), jnp.float32),
            pltpu.VMEM((1, 4, 2048), jnp.bfloat16),
            pltpu.VMEM((2 * OWNERS, LANES), jnp.float32),
            pltpu.SemaphoreType.DMA((4,)),
            pltpu.SemaphoreType.DMA((K_MAX,)),
        ],
        compiler_params=pltpu.CompilerParams(vmem_limit_bytes=20 * MIB),
        name="forward",
    )(
        in_hbm(block_ids),
        in_hbm(offsets),
        counts,
        in_hbm(image),
        in_hbm(weights),
        in_hbm(measured),
    )
    got = lax.all_to_all(sent, VOX, 0, 0, tiled=True)
    sent, resid = pl.pallas_call(
        owner_kernel,
        out_shape=(
            jax.ShapeDtypeStruct((OWNERS, 2, WIDTH), jnp.bfloat16),
            jax.ShapeDtypeStruct((64, LANES), jnp.float32),
        ),
        in_specs=[vmem(), vmem()],
        out_specs=(vmem(), vmem()),
        scratch_shapes=[pltpu.VMEM((2 * OWNERS, WIDTH), jnp.float32)],
        compiler_params=pltpu.CompilerParams(vmem_limit_bytes=8 * MIB),
        name="owner",
    )(got, spread)
    got = lax.all_to_all(sent, VOX, 0, 0, tiled=True)
    grad = pl.pallas_call(
        backward_kernel,
        out_shape=jax.ShapeDtypeStruct((1, 2, 512), jnp.float32),
        in_specs=[vmem(), vmem(), vmem()],
        out_specs=vmem(),
        scratch_shapes=[pltpu.VMEM((K_MAX, 8, LANES), jnp.float32)],
        compiler_params=pltpu.CompilerParams(vmem_limit_bytes=20 * MIB),
        name="backward",
    )(places, got, held)
    grad = grad + lax.ppermute(grad, "core", [(0, 1), (1, 0)])
    other = lax.ppermute(grad, "z_hi", [(0, 1), (1, 0)])
    base, residual = pl.pallas_call(
        smooth_kernel,
        out_shape=(
            jax.ShapeDtypeStruct((1, 2, 512), jnp.float32),
            jax.ShapeDtypeStruct((1, 4, 2048), jnp.float32),
        ),
        in_specs=[vmem(), vmem(), vmem()],
        out_specs=(vmem(), vmem()),
        scratch_shapes=[pltpu.VMEM((2 * OWNERS, LANES), jnp.float32)],
        compiler_params=pltpu.CompilerParams(vmem_limit_bytes=8 * MIB),
        cost_estimate=pl.CostEstimate(flops=100000, bytes_accessed=1 << 19, transcendentals=4096),
        name="smooth",
    )(got, image, resid)
    return (base - STEP_SIZE * (grad + other), residual)


def solution(mesh):
    fine = Mesh(mesh.devices.reshape(4, 4, 4, 2, 2), VOX + SEN)
    placed = (
        P(VOX, None, None),
        P(VOX, SEN, None, None, None),
        P(VOX, SEN, None),
        P(VOX, SEN, None),
        P(VOX, SEN),
        P(SEN, VOX, None),
    )
    return jax.shard_map(
        on_device,
        mesh=fine,
        in_specs=placed,
        out_specs=(P(VOX, None, None), P(SEN, VOX, None)),
        check_vma=False,
    )
```

```python
import functools

import jax
import jax.numpy as jnp
from jax import lax
from jax.experimental import pallas as pl
from jax.experimental.pallas import tpu as pltpu
from jax.sharding import Mesh
from jax.sharding import PartitionSpec as P

SB = 16
WIN = 64
K_MAX = 5
VOXELS = 1024
CELLS = SB * WIN
LANES = 128
TILES = K_MAX + 1
WIDTH = TILES * LANES
OWNERS = 64
ON_MATRIX = 2
AHEAD = 2
PLACE = 2048
LIVE = 16 * PLACE
STEP_SIZE = 0.25
TV_WEIGHT = 0.3
TV_EPS = 0.01
NOWHERE = 255.0
MIB = 1 << 20

VOX = ("y", "x", "z_lo")
SEN = ("z_hi", "core")


def lane_iota(shape):
    return lax.broadcasted_iota(jnp.int32, shape, len(shape) - 1)


def as_tile(image):
    rows = [image[0, y : y + 1, t * LANES : (t + 1) * LANES] for y in range(2) for t in range(4)]
    return jnp.concatenate(rows, axis=0)


def split_three(x):
    parts = []
    for _ in range(3):
        part = x.astype(jnp.bfloat16).astype(jnp.float32)
        parts.append(part)
        x = x - part
    return parts


def forward_kernel(
    ids_hbm,
    starts_hbm,
    counts,
    image_hbm,
    weights,
    measured_hbm,
    sent,
    spread,
    held,
    places,
    ids,
    starts,
    image,
    measured,
    halo,
    small_sems,
    sems,
):
    small = []
    for i, (src, dst) in enumerate(
        (
            (image_hbm, image),
            (ids_hbm, ids),
            (starts_hbm, starts),
            (measured_hbm, measured),
        )
    ):
        small.append(pltpu.make_async_copy(src, dst, small_sems.at[i]))
        small[-1].start()
    copies = [
        pltpu.make_async_copy(weights.at[0, 0, k], held.at[k], sems.at[k]) for k in range(K_MAX)
    ]
    for k in range(K_MAX):
        copies[k].start(priority=0 if k < AHEAD else 1)
    for copy in small:
        copy.wait()

    own = measured[0].astype(jnp.float32)
    for r in range(4):
        for h in range(16):
            spread[r * 16 + h : r * 16 + h + 1, :] = own[r : r + 1, h * LANES : (h + 1) * LANES]

    plane = as_tile(image)
    turned = jnp.concatenate(split_three(plane) + [jnp.zeros((104, LANES), jnp.float32)], axis=0).T
    halo[...] = pltpu.roll(turned, 32, 1)

    voxels = jnp.concatenate([image[0, 0:1, :], image[0, 1:2, :]], axis=1).astype(jnp.bfloat16)
    lane2 = lane_iota((2, LANES))
    base = jnp.full((2, LANES), NOWHERE, jnp.float32)
    code_row = base
    block_row = jnp.full((2, LANES), -1, jnp.int32)
    live = counts[0, 0]
    table = jnp.zeros((8, LANES), jnp.int32)
    for k in range(K_MAX):
        start = starts[0, 0, k]
        place = start + ids[0, 0, k] * PLACE + jnp.where(k < live, LIVE, 0)
        table = jnp.where(lane_iota((8, LANES)) == k, place, table)
        coarse = start // WIN
        low = start - coarse * WIN
        code = (coarse & 1) * 16 + (coarse >> 1)
        block = jnp.where(k < live, ids[0, 0, k], -1)
        base = jnp.where(lane2 == 8 + k, low.astype(jnp.float32), base)
        code_row = jnp.where(lane2 == k, code.astype(jnp.float32), code_row)
        block_row = jnp.where(lane2 == k, block, block_row)
    places[...] = table
    for b in range(16):
        marked = jnp.where(block_row == b, code_row, base)
        for d in range(4 * b, 4 * b + 4):
            own_halo = halo[pl.ds(d, 2, stride=OWNERS), :]
            sent[d, :, K_MAX * LANES :] = jnp.where(lane2 < 32, marked, own_halo).astype(
                jnp.bfloat16
            )

    lane = lane_iota((8, LANES))
    for k in range(K_MAX):
        copies[k].wait()
        piece = jnp.dot(voxels, held[k], preferred_element_type=jnp.float32)
        tile = jnp.concatenate([piece[:, i * LANES : (i + 1) * LANES] for i in range(8)], axis=0)
        low = lax.rem(starts[0, 0, k], WIN)
        tile = jnp.where(
            (lane & (WIN - 1)) >= low, pltpu.roll(tile, low, 1), pltpu.roll(tile, low + WIN, 1)
        )
        for q in range(4):
            strip = tile[2 * q : 2 * q + 2, :].astype(jnp.bfloat16)
            for b in range(16):
                sent[4 * b + q, :, k * LANES : (k + 1) * LANES] = strip


def derivative(x):
    row = lax.broadcasted_iota(jnp.int32, x.shape, 0) & 15
    lane = lane_iota(x.shape)

    following = jnp.where(row == 15, 0.0, pltpu.roll(x, x.shape[0] - 1, 0))
    previous = jnp.where(row == 0, 0.0, pltpu.roll(x, 1, 0))

    def ahead(t):
        return pltpu.roll(jnp.where(lane < t, following, x), LANES - t, 1)

    def behind(t):
        return pltpu.roll(jnp.where(lane >= LANES - t, previous, x), t, 1)

    return ((behind(2) - ahead(2)) + 8.0 * (ahead(1) - behind(1))) * (1.0 / 12.0)


def owner_kernel(got, spread, sent, resid, wide):
    wide[...] = got[...].reshape(2 * OWNERS, WIDTH).astype(jnp.float32)
    lane = lane_iota((LANES, LANES))
    parity = lax.broadcasted_iota(jnp.int32, (LANES, LANES), 0) & 1
    within = (lane & (WIN - 1)).astype(jnp.float32)
    own_half = (lane >> 6) == parity
    first_half = (lane & 32) == 0
    slot = jnp.where(own_half, lane & 31, -1).astype(jnp.float32)
    info = wide[:, K_MAX * LANES :]
    shape = (LANES, 2 * K_MAX * LANES)
    source = lax.broadcasted_iota(jnp.int32, shape, 1) >> 7
    source = jnp.where(source < K_MAX, source, source + 8 - K_MAX)
    pick = jnp.where(lax.broadcasted_iota(jnp.int32, shape, 0) == source, 1.0, 0.0)
    spread_out = jnp.dot(
        jnp.where(lane < 16, info, 0.0).astype(jnp.bfloat16),
        pick.astype(jnp.bfloat16),
        preferred_element_type=jnp.float32,
    )
    places, strips, later = [], [], []
    for k in range(K_MAX):
        code = spread_out[:, k * LANES : (k + 1) * LANES]
        low = spread_out[:, (K_MAX + k) * LANES : (K_MAX + k + 1) * LANES]
        following = jnp.where(code >= 16.0, code - 15.0, code + 16.0)
        wanted = jnp.where(first_half, code, following)
        places.append(jnp.where(wanted == slot, 1.0, 0.0))
        first = within >= low
        later.append(first)
        strip = wide[:, k * LANES : (k + 1) * LANES]
        strips.append(
            jnp.concatenate([jnp.where(first, strip, 0.0), jnp.where(first, 0.0, strip)], axis=1)
        )
    place = jnp.concatenate(places, axis=0).astype(jnp.bfloat16)
    strip = jnp.concatenate(strips, axis=0).astype(jnp.bfloat16)
    both = lax.dot_general(
        place, strip, (((0,), (0,)), ((), ())), preferred_element_type=jnp.float32
    )
    lane16 = lane_iota((16, LANES)) < WIN
    rows = []
    for u in range(2):
        summed = both[64 * u : 64 * u + 32, :LANES] + both[64 * u + 32 : 64 * u + 64, LANES:]
        even = summed[0:16]
        odd = summed[16:32]
        rows.append(jnp.where(lane16, even, pltpu.roll(odd, WIN, 1)))
        rows.append(jnp.where(lane16, pltpu.roll(even, WIN, 1), odd))
    signals = jnp.concatenate(rows, axis=0)
    difference = derivative(signals) - spread[...]
    resid[...] = difference
    adjoint = -derivative(difference)
    zero = jnp.zeros((32, LANES), jnp.float32)
    table = []
    for u in range(2):
        a = adjoint[32 * u : 32 * u + 16]
        b = adjoint[32 * u + 16 : 32 * u + 32]
        half = jnp.concatenate(
            [
                jnp.where(lane16, a, pltpu.roll(b, WIN, 1)),
                jnp.where(lane16, pltpu.roll(a, WIN, 1), b),
            ],
            axis=0,
        )
        table.append(jnp.concatenate([half, zero], axis=1))
        table.append(jnp.concatenate([zero, half], axis=1))
    table = jnp.concatenate(table, axis=0).astype(jnp.bfloat16)
    cut = jnp.dot(place, table, preferred_element_type=jnp.float32)
    for k in range(K_MAX):
        mine = cut[k * LANES : (k + 1) * LANES]
        wide[:, k * LANES : (k + 1) * LANES] = jnp.where(
            later[k], mine[:, :LANES], mine[:, LANES:]
        )
    wide[:, K_MAX * LANES :] = jnp.where(
        lane < WIN,
        pltpu.roll(info, 2, 0),
        pltpu.roll(pltpu.roll(info, LANES - 2, 0), 32, 1),
    )
    sent[...] = wide[...].astype(jnp.bfloat16).reshape(OWNERS, 2, WIDTH)


def total_variation(image, before, after, is_first, is_last):
    lane = lane_iota((8, LANES))
    row = lax.broadcasted_iota(jnp.int32, (8, LANES), 0)
    last_x = (lane == LANES - 1) & ((row & 3) == 3)
    first_x = (lane == 0) & ((row & 3) == 0)

    def units(here, ahead, no_step):
        step_z = jnp.where(no_step, 0.0, ahead - here)
        step_y = jnp.where(row >= 4, 0.0, pltpu.roll(here, 4, 0) - here)
        moved = pltpu.roll(here, LANES - 1, 1)
        moved = jnp.where(lane == LANES - 1, pltpu.roll(moved, 7, 0), moved)
        step_x = jnp.where(last_x, 0.0, moved - here)
        magnitude = jnp.sqrt(step_z * step_z + step_y * step_y + step_x * step_x + TV_EPS)
        return step_z / magnitude, step_y / magnitude, step_x / magnitude

    unit_z, unit_y, unit_x = units(image, after, is_last)
    below_z, _, _ = units(before, image, is_first)
    result = below_z - unit_z
    result = result + (jnp.where(row < 4, 0.0, pltpu.roll(unit_y, 4, 0)) - unit_y)
    moved = pltpu.roll(unit_x, 1, 1)
    moved = jnp.where(lane == 0, pltpu.roll(moved, 1, 0), moved)
    return result + (jnp.where(first_x, 0.0, moved) - unit_x)


def smooth_kernel(got, image, resid, base, residual, wide):
    for r in range(4):
        for h in range(16):
            residual[0, r : r + 1, h * LANES : (h + 1) * LANES] = resid[
                r * 16 + h : r * 16 + h + 1, :
            ]
    vox = lax.axis_index(VOX)
    for d in range(OWNERS):
        wide[2 * d : 2 * d + 2, :] = got[d, :, K_MAX * LANES :].astype(jnp.float32)
    shard = jnp.concatenate([wide[pl.ds(u, OWNERS, stride=2), :] for u in range(2)], axis=0)
    whole = shard + (pltpu.roll(shard, LANES - 8, 1) + pltpu.roll(shard, LANES - 16, 1))
    turned = whole.T
    here = as_tile(image)
    tv = total_variation(here, turned[32:40], turned[64:72], vox == 0, vox == OWNERS - 1)
    out = here - (STEP_SIZE * TV_WEIGHT) * tv
    for y in range(2):
        for t in range(4):
            base[0, y : y + 1, t * LANES : (t + 1) * LANES] = out[y * 4 + t : y * 4 + t + 1]


def backward_kernel(table, got, held, grad, wins):
    lane = lane_iota((8, LANES))
    places = [table[0, k] for k in range(K_MAX)]
    for k in range(K_MAX):
        block = (places[k] >> 11) & 15
        for q in range(4):
            strip = got[4 * block + q, :, k * LANES : (k + 1) * LANES]
            wins[k, 2 * q : 2 * q + 2, :] = strip.astype(jnp.float32)
    windows = []
    for k in range(K_MAX):
        low = places[k] & (WIN - 1)
        tile = wins[k]
        tile = jnp.where(
            (lane & (WIN - 1)) < WIN - low,
            pltpu.roll(tile, lax.rem(LANES - low, LANES), 1),
            pltpu.roll(tile, WIN - low, 1),
        )
        windows.append(jnp.where(places[k] >= LIVE, tile, 0.0))
    vectors = [
        jnp.concatenate([windows[k][i : i + 1, :] for i in range(8)], axis=1).astype(jnp.bfloat16)
        for k in range(ON_MATRIX)
    ]
    for j in range(8):
        rows = slice(j * LANES, (j + 1) * LANES)
        total = jnp.zeros((1, LANES), jnp.float32)
        for k in range(ON_MATRIX):
            total = total + lax.dot_general(
                vectors[k],
                held[k, rows, :],
                (((1,), (1,)), ((), ())),
                preferred_element_type=jnp.float32,
            )
        partial = jnp.zeros((LANES, LANES), jnp.float32)
        for k in range(ON_MATRIX, K_MAX):
            block = held[k, rows, :].astype(jnp.float32)
            for i in range(8):
                weight = jnp.broadcast_to(windows[k][i : i + 1, :], (LANES, LANES))
                partial = partial + block[:, i * LANES : (i + 1) * LANES] * weight
        total = total + jnp.sum(partial.T, axis=0, keepdims=True)
        y, t = j // 4, j % 4
        grad[0, y : y + 1, t * LANES : (t + 1) * LANES] = total


def smem():
    return pl.BlockSpec(memory_space=pltpu.SMEM)


def vmem():
    return pl.BlockSpec(memory_space=pltpu.VMEM)


def hbm():
    return pl.BlockSpec(memory_space=pltpu.HBM)


def in_hbm(array):
    return pltpu.with_memory_space_constraint(array, pltpu.HBM)


def on_device(image, weights, block_ids, offsets, counts, measured):
    sent, spread, held, places = pl.pallas_call(
        forward_kernel,
        out_shape=(
            jax.ShapeDtypeStruct((OWNERS, 2, WIDTH), jnp.bfloat16),
            jax.ShapeDtypeStruct((64, LANES), jnp.float32),
            jax.ShapeDtypeStruct((K_MAX, VOXELS, CELLS), jnp.bfloat16),
            jax.ShapeDtypeStruct((8, LANES), jnp.int32),
        ),
        in_specs=[hbm(), hbm(), smem(), hbm(), hbm(), hbm()],
        out_specs=(vmem(),) * 4,
        scratch_shapes=[
            pltpu.SMEM((1, 1, K_MAX), jnp.int32),
            pltpu.SMEM((1, 1, K_MAX), jnp.int32),
            pltpu.VMEM((1, 2, 512), jnp.float32),
            pltpu.VMEM((1, 4, 2048), jnp.bfloat16),
            pltpu.VMEM((2 * OWNERS, LANES), jnp.float32),
            pltpu.SemaphoreType.DMA((4,)),
            pltpu.SemaphoreType.DMA((K_MAX,)),
        ],
        compiler_params=pltpu.CompilerParams(vmem_limit_bytes=20 * MIB),
        name="forward",
    )(
        in_hbm(block_ids),
        in_hbm(offsets),
        counts,
        in_hbm(image),
        in_hbm(weights),
        in_hbm(measured),
    )
    got = lax.all_to_all(sent, VOX, 0, 0, tiled=True)
    sent, resid = pl.pallas_call(
        owner_kernel,
        out_shape=(
            jax.ShapeDtypeStruct((OWNERS, 2, WIDTH), jnp.bfloat16),
            jax.ShapeDtypeStruct((64, LANES), jnp.float32),
        ),
        in_specs=[vmem(), vmem()],
        out_specs=(vmem(), vmem()),
        scratch_shapes=[pltpu.VMEM((2 * OWNERS, WIDTH), jnp.float32)],
        compiler_params=pltpu.CompilerParams(vmem_limit_bytes=8 * MIB),
        name="owner",
    )(got, spread)
    got = lax.all_to_all(sent, VOX, 0, 0, tiled=True)
    grad = pl.pallas_call(
        backward_kernel,
        out_shape=jax.ShapeDtypeStruct((1, 2, 512), jnp.float32),
        in_specs=[vmem(), vmem(), vmem()],
        out_specs=vmem(),
        scratch_shapes=[pltpu.VMEM((K_MAX, 8, LANES), jnp.float32)],
        compiler_params=pltpu.CompilerParams(vmem_limit_bytes=20 * MIB),
        name="backward",
    )(places, got, held)
    grad = grad + lax.ppermute(grad, "core", [(0, 1), (1, 0)])
    other = lax.ppermute(grad, "z_hi", [(0, 1), (1, 0)])
    base, residual = pl.pallas_call(
        smooth_kernel,
        out_shape=(
            jax.ShapeDtypeStruct((1, 2, 512), jnp.float32),
            jax.ShapeDtypeStruct((1, 4, 2048), jnp.float32),
        ),
        in_specs=[vmem(), vmem(), vmem()],
        out_specs=(vmem(), vmem()),
        scratch_shapes=[pltpu.VMEM((2 * OWNERS, LANES), jnp.float32)],
        compiler_params=pltpu.CompilerParams(vmem_limit_bytes=8 * MIB),
        cost_estimate=pl.CostEstimate(flops=100000, bytes_accessed=1 << 19, transcendentals=4096),
        name="smooth",
    )(got, image, resid)
    return (base - STEP_SIZE * (grad + other), residual)


def solution(mesh):
    fine = Mesh(mesh.devices.reshape(4, 4, 4, 2, 2), VOX + SEN)
    placed = (
        P(VOX, None, None),
        P(VOX, SEN, None, None, None),
        P(VOX, SEN, None),
        P(VOX, SEN, None),
        P(VOX, SEN),
        P(SEN, VOX, None),
    )
    return jax.shard_map(
        on_device,
        mesh=fine,
        in_specs=placed,
        out_specs=(P(VOX, None, None), P(SEN, VOX, None)),
        check_vma=False,
    )
```

```python
import functools

import jax
import jax.numpy as jnp
from jax import lax
from jax.experimental import pallas as pl
from jax.experimental.pallas import tpu as pltpu
from jax.sharding import Mesh
from jax.sharding import PartitionSpec as P

SB = 16
WIN = 64
K_MAX = 5
VOXELS = 1024
CELLS = SB * WIN
LANES = 128
TILES = K_MAX + 1
WIDTH = TILES * LANES
OWNERS = 64
ON_MATRIX = 2
AHEAD = 1
PLACE = 2048
LIVE = 16 * PLACE
STEP_SIZE = 0.25
TV_WEIGHT = 0.3
TV_EPS = 0.01
NOWHERE = 255.0
MIB = 1 << 20

VOX = ("y", "x", "z_lo")
SEN = ("z_hi", "core")


def lane_iota(shape):
    return lax.broadcasted_iota(jnp.int32, shape, len(shape) - 1)


def as_tile(image):
    rows = [image[0, y : y + 1, t * LANES : (t + 1) * LANES] for y in range(2) for t in range(4)]
    return jnp.concatenate(rows, axis=0)


def split_three(x):
    parts = []
    for _ in range(3):
        part = x.astype(jnp.bfloat16).astype(jnp.float32)
        parts.append(part)
        x = x - part
    return parts


def forward_kernel(
    ids_hbm,
    starts_hbm,
    counts,
    image_hbm,
    weights,
    measured_hbm,
    sent,
    spread,
    held,
    places,
    ids,
    starts,
    image,
    measured,
    halo,
    small_sems,
    sems,
):
    small = []
    for i, (src, dst) in enumerate(
        (
            (image_hbm, image),
            (ids_hbm, ids),
            (starts_hbm, starts),
            (measured_hbm, measured),
        )
    ):
        small.append(pltpu.make_async_copy(src, dst, small_sems.at[i]))
        small[-1].start()
    copies = [
        pltpu.make_async_copy(weights.at[0, 0, k], held.at[k], sems.at[k]) for k in range(K_MAX)
    ]
    for k in range(K_MAX):
        copies[k].start(priority=0 if k < AHEAD else 1)
    for copy in small:
        copy.wait()

    own = measured[0].astype(jnp.float32)
    for r in range(4):
        for h in range(16):
            spread[r * 16 + h : r * 16 + h + 1, :] = own[r : r + 1, h * LANES : (h + 1) * LANES]

    plane = as_tile(image)
    turned = jnp.concatenate(split_three(plane) + [jnp.zeros((104, LANES), jnp.float32)], axis=0).T
    halo[...] = pltpu.roll(turned, 32, 1)

    voxels = jnp.concatenate([image[0, 0:1, :], image[0, 1:2, :]], axis=1).astype(jnp.bfloat16)
    lane2 = lane_iota((2, LANES))
    base = jnp.full((2, LANES), NOWHERE, jnp.float32)
    code_row = base
    block_row = jnp.full((2, LANES), -1, jnp.int32)
    live = counts[0, 0]
    table = jnp.zeros((8, LANES), jnp.int32)
    for k in range(K_MAX):
        start = starts[0, 0, k]
        place = start + ids[0, 0, k] * PLACE + jnp.where(k < live, LIVE, 0)
        table = jnp.where(lane_iota((8, LANES)) == k, place, table)
        coarse = start // WIN
        low = start - coarse * WIN
        code = (coarse & 1) * 16 + (coarse >> 1)
        block = jnp.where(k < live, ids[0, 0, k], -1)
        base = jnp.where(lane2 == 8 + k, low.astype(jnp.float32), base)
        code_row = jnp.where(lane2 == k, code.astype(jnp.float32), code_row)
        block_row = jnp.where(lane2 == k, block, block_row)
    places[...] = table
    for b in range(16):
        marked = jnp.where(block_row == b, code_row, base)
        for d in range(4 * b, 4 * b + 4):
            own_halo = halo[pl.ds(d, 2, stride=OWNERS), :]
            sent[d, :, K_MAX * LANES :] = jnp.where(lane2 < 32, marked, own_halo).astype(
                jnp.bfloat16
            )

    lane = lane_iota((8, LANES))
    for k in range(K_MAX):
        copies[k].wait()
        piece = jnp.dot(voxels, held[k], preferred_element_type=jnp.float32)
        tile = jnp.concatenate([piece[:, i * LANES : (i + 1) * LANES] for i in range(8)], axis=0)
        low = lax.rem(starts[0, 0, k], WIN)
        tile = jnp.where(
            (lane & (WIN - 1)) >= low, pltpu.roll(tile, low, 1), pltpu.roll(tile, low + WIN, 1)
        )
        for q in range(4):
            strip = tile[2 * q : 2 * q + 2, :].astype(jnp.bfloat16)
            for b in range(16):
                sent[4 * b + q, :, k * LANES : (k + 1) * LANES] = strip


def derivative(x):
    row = lax.broadcasted_iota(jnp.int32, x.shape, 0) & 15
    lane = lane_iota(x.shape)

    def ahead(t):
        rolled = pltpu.roll(x, LANES - t, 1)
        after = jnp.where(row == 15, 0.0, pltpu.roll(rolled, x.shape[0] - 1, 0))
        return jnp.where(lane >= LANES - t, after, rolled)

    def behind(t):
        rolled = pltpu.roll(x, t, 1)
        before = jnp.where(row == 0, 0.0, pltpu.roll(rolled, 1, 0))
        return jnp.where(lane < t, before, rolled)

    return ((behind(2) - ahead(2)) + 8.0 * (ahead(1) - behind(1))) * (1.0 / 12.0)


def owner_kernel(got, spread, sent, resid, wide):
    wide[...] = got[...].reshape(2 * OWNERS, WIDTH).astype(jnp.float32)
    lane = lane_iota((LANES, LANES))
    parity = lax.broadcasted_iota(jnp.int32, (LANES, LANES), 0) & 1
    within = (lane & (WIN - 1)).astype(jnp.float32)
    own_half = (lane >> 6) == parity
    first_half = (lane & 32) == 0
    slot = jnp.where(own_half, lane & 31, -1).astype(jnp.float32)
    info = wide[:, K_MAX * LANES :]
    shape = (LANES, 2 * K_MAX * LANES)
    source = lax.broadcasted_iota(jnp.int32, shape, 1) >> 7
    source = jnp.where(source < K_MAX, source, source + 8 - K_MAX)
    pick = jnp.where(lax.broadcasted_iota(jnp.int32, shape, 0) == source, 1.0, 0.0)
    spread_out = jnp.dot(
        jnp.where(lane < 16, info, 0.0).astype(jnp.bfloat16),
        pick.astype(jnp.bfloat16),
        preferred_element_type=jnp.float32,
    )
    places, strips, later = [], [], []
    for k in range(K_MAX):
        code = spread_out[:, k * LANES : (k + 1) * LANES]
        low = spread_out[:, (K_MAX + k) * LANES : (K_MAX + k + 1) * LANES]
        following = jnp.where(code >= 16.0, code - 15.0, code + 16.0)
        wanted = jnp.where(first_half, code, following)
        places.append(jnp.where(wanted == slot, 1.0, 0.0))
        first = within >= low
        later.append(first)
        strip = wide[:, k * LANES : (k + 1) * LANES]
        strips.append(
            jnp.concatenate([jnp.where(first, strip, 0.0), jnp.where(first, 0.0, strip)], axis=1)
        )
    place = jnp.concatenate(places, axis=0).astype(jnp.bfloat16)
    strip = jnp.concatenate(strips, axis=0).astype(jnp.bfloat16)
    both = lax.dot_general(
        place, strip, (((0,), (0,)), ((), ())), preferred_element_type=jnp.float32
    )
    lane16 = lane_iota((16, LANES)) < WIN
    rows = []
    for u in range(2):
        summed = both[64 * u : 64 * u + 32, :LANES] + both[64 * u + 32 : 64 * u + 64, LANES:]
        even = summed[0:16]
        odd = summed[16:32]
        rows.append(jnp.where(lane16, even, pltpu.roll(odd, WIN, 1)))
        rows.append(jnp.where(lane16, pltpu.roll(even, WIN, 1), odd))
    signals = jnp.concatenate(rows, axis=0)
    difference = derivative(signals) - spread[...]
    resid[...] = difference
    adjoint = -derivative(difference)
    zero = jnp.zeros((32, LANES), jnp.float32)
    table = []
    for u in range(2):
        a = adjoint[32 * u : 32 * u + 16]
        b = adjoint[32 * u + 16 : 32 * u + 32]
        half = jnp.concatenate(
            [
                jnp.where(lane16, a, pltpu.roll(b, WIN, 1)),
                jnp.where(lane16, pltpu.roll(a, WIN, 1), b),
            ],
            axis=0,
        )
        table.append(jnp.concatenate([half, zero], axis=1))
        table.append(jnp.concatenate([zero, half], axis=1))
    table = jnp.concatenate(table, axis=0).astype(jnp.bfloat16)
    cut = jnp.dot(place, table, preferred_element_type=jnp.float32)
    for k in range(K_MAX):
        mine = cut[k * LANES : (k + 1) * LANES]
        wide[:, k * LANES : (k + 1) * LANES] = jnp.where(
            later[k], mine[:, :LANES], mine[:, LANES:]
        )
    wide[:, K_MAX * LANES :] = jnp.where(
        lane < WIN,
        pltpu.roll(info, 2, 0),
        pltpu.roll(pltpu.roll(info, LANES - 2, 0), 32, 1),
    )
    sent[...] = wide[...].astype(jnp.bfloat16).reshape(OWNERS, 2, WIDTH)


def total_variation(image, before, after, is_first, is_last):
    lane = lane_iota((8, LANES))
    row = lax.broadcasted_iota(jnp.int32, (8, LANES), 0)
    last_x = (lane == LANES - 1) & ((row & 3) == 3)
    first_x = (lane == 0) & ((row & 3) == 0)

    def units(here, ahead, no_step):
        step_z = jnp.where(no_step, 0.0, ahead - here)
        step_y = jnp.where(row >= 4, 0.0, pltpu.roll(here, 4, 0) - here)
        moved = pltpu.roll(here, LANES - 1, 1)
        moved = jnp.where(lane == LANES - 1, pltpu.roll(moved, 7, 0), moved)
        step_x = jnp.where(last_x, 0.0, moved - here)
        magnitude = jnp.sqrt(step_z * step_z + step_y * step_y + step_x * step_x + TV_EPS)
        return step_z / magnitude, step_y / magnitude, step_x / magnitude

    unit_z, unit_y, unit_x = units(image, after, is_last)
    below_z, _, _ = units(before, image, is_first)
    result = below_z - unit_z
    result = result + (jnp.where(row < 4, 0.0, pltpu.roll(unit_y, 4, 0)) - unit_y)
    moved = pltpu.roll(unit_x, 1, 1)
    moved = jnp.where(lane == 0, pltpu.roll(moved, 1, 0), moved)
    return result + (jnp.where(first_x, 0.0, moved) - unit_x)


def smooth_kernel(got, image, resid, base, residual, wide):
    for r in range(4):
        for h in range(16):
            residual[0, r : r + 1, h * LANES : (h + 1) * LANES] = resid[
                r * 16 + h : r * 16 + h + 1, :
            ]
    vox = lax.axis_index(VOX)
    for d in range(OWNERS):
        wide[2 * d : 2 * d + 2, :] = got[d, :, K_MAX * LANES :].astype(jnp.float32)
    shard = jnp.concatenate([wide[pl.ds(u, OWNERS, stride=2), :] for u in range(2)], axis=0)
    whole = shard + (pltpu.roll(shard, LANES - 8, 1) + pltpu.roll(shard, LANES - 16, 1))
    turned = whole.T
    here = as_tile(image)
    tv = total_variation(here, turned[32:40], turned[64:72], vox == 0, vox == OWNERS - 1)
    out = here - (STEP_SIZE * TV_WEIGHT) * tv
    for y in range(2):
        for t in range(4):
            base[0, y : y + 1, t * LANES : (t + 1) * LANES] = out[y * 4 + t : y * 4 + t + 1]


def backward_kernel(table, got, held, grad, wins):
    lane = lane_iota((8, LANES))
    places = [table[0, k] for k in range(K_MAX)]
    for k in range(K_MAX):
        block = (places[k] >> 11) & 15
        for q in range(4):
            strip = got[4 * block + q, :, k * LANES : (k + 1) * LANES]
            wins[k, 2 * q : 2 * q + 2, :] = strip.astype(jnp.float32)
    windows = []
    for k in range(K_MAX):
        low = places[k] & (WIN - 1)
        tile = wins[k]
        tile = jnp.where(
            (lane & (WIN - 1)) < WIN - low,
            pltpu.roll(tile, lax.rem(LANES - low, LANES), 1),
            pltpu.roll(tile, WIN - low, 1),
        )
        windows.append(jnp.where(places[k] >= LIVE, tile, 0.0))
    vectors = [
        jnp.concatenate([windows[k][i : i + 1, :] for i in range(8)], axis=1).astype(jnp.bfloat16)
        for k in range(ON_MATRIX)
    ]
    for j in range(8):
        rows = slice(j * LANES, (j + 1) * LANES)
        total = jnp.zeros((1, LANES), jnp.float32)
        for k in range(ON_MATRIX):
            total = total + lax.dot_general(
                vectors[k],
                held[k, rows, :],
                (((1,), (1,)), ((), ())),
                preferred_element_type=jnp.float32,
            )
        partial = jnp.zeros((LANES, LANES), jnp.float32)
        for k in range(ON_MATRIX, K_MAX):
            block = held[k, rows, :].astype(jnp.float32)
            for i in range(8):
                weight = jnp.broadcast_to(windows[k][i : i + 1, :], (LANES, LANES))
                partial = partial + block[:, i * LANES : (i + 1) * LANES] * weight
        total = total + jnp.sum(partial.T, axis=0, keepdims=True)
        y, t = j // 4, j % 4
        grad[0, y : y + 1, t * LANES : (t + 1) * LANES] = total


def smem():
    return pl.BlockSpec(memory_space=pltpu.SMEM)


def vmem():
    return pl.BlockSpec(memory_space=pltpu.VMEM)


def hbm():
    return pl.BlockSpec(memory_space=pltpu.HBM)


def in_hbm(array):
    return pltpu.with_memory_space_constraint(array, pltpu.HBM)


def on_device(image, weights, block_ids, offsets, counts, measured):
    sent, spread, held, places = pl.pallas_call(
        forward_kernel,
        out_shape=(
            jax.ShapeDtypeStruct((OWNERS, 2, WIDTH), jnp.bfloat16),
            jax.ShapeDtypeStruct((64, LANES), jnp.float32),
            jax.ShapeDtypeStruct((K_MAX, VOXELS, CELLS), jnp.bfloat16),
            jax.ShapeDtypeStruct((8, LANES), jnp.int32),
        ),
        in_specs=[hbm(), hbm(), smem(), hbm(), hbm(), hbm()],
        out_specs=(vmem(),) * 4,
        scratch_shapes=[
            pltpu.SMEM((1, 1, K_MAX), jnp.int32),
            pltpu.SMEM((1, 1, K_MAX), jnp.int32),
            pltpu.VMEM((1, 2, 512), jnp.float32),
            pltpu.VMEM((1, 4, 2048), jnp.bfloat16),
            pltpu.VMEM((2 * OWNERS, LANES), jnp.float32),
            pltpu.SemaphoreType.DMA((4,)),
            pltpu.SemaphoreType.DMA((K_MAX,)),
        ],
        compiler_params=pltpu.CompilerParams(vmem_limit_bytes=20 * MIB),
        name="forward",
    )(
        in_hbm(block_ids),
        in_hbm(offsets),
        counts,
        in_hbm(image),
        in_hbm(weights),
        in_hbm(measured),
    )
    got = lax.all_to_all(sent, VOX, 0, 0, tiled=True)
    sent, resid = pl.pallas_call(
        owner_kernel,
        out_shape=(
            jax.ShapeDtypeStruct((OWNERS, 2, WIDTH), jnp.bfloat16),
            jax.ShapeDtypeStruct((64, LANES), jnp.float32),
        ),
        in_specs=[vmem(), vmem()],
        out_specs=(vmem(), vmem()),
        scratch_shapes=[pltpu.VMEM((2 * OWNERS, WIDTH), jnp.float32)],
        compiler_params=pltpu.CompilerParams(vmem_limit_bytes=8 * MIB),
        name="owner",
    )(got, spread)
    got = lax.all_to_all(sent, VOX, 0, 0, tiled=True)
    grad = pl.pallas_call(
        backward_kernel,
        out_shape=jax.ShapeDtypeStruct((1, 2, 512), jnp.float32),
        in_specs=[vmem(), vmem(), vmem()],
        out_specs=vmem(),
        scratch_shapes=[pltpu.VMEM((K_MAX, 8, LANES), jnp.float32)],
        compiler_params=pltpu.CompilerParams(vmem_limit_bytes=20 * MIB),
        name="backward",
    )(places, got, held)
    grad = grad + lax.ppermute(grad, "core", [(0, 1), (1, 0)])
    other = lax.ppermute(grad, "z_hi", [(0, 1), (1, 0)])
    base, residual = pl.pallas_call(
        smooth_kernel,
        out_shape=(
            jax.ShapeDtypeStruct((1, 2, 512), jnp.float32),
            jax.ShapeDtypeStruct((1, 4, 2048), jnp.float32),
        ),
        in_specs=[vmem(), vmem(), vmem()],
        out_specs=(vmem(), vmem()),
        scratch_shapes=[pltpu.VMEM((2 * OWNERS, LANES), jnp.float32)],
        compiler_params=pltpu.CompilerParams(vmem_limit_bytes=8 * MIB),
        cost_estimate=pl.CostEstimate(flops=100000, bytes_accessed=1 << 19, transcendentals=4096),
        name="smooth",
    )(got, image, resid)
    return (base - STEP_SIZE * (grad + other), residual)


def solution(mesh):
    fine = Mesh(mesh.devices.reshape(4, 4, 4, 2, 2), VOX + SEN)
    placed = (
        P(VOX, None, None),
        P(VOX, SEN, None, None, None),
        P(VOX, SEN, None),
        P(VOX, SEN, None),
        P(VOX, SEN),
        P(SEN, VOX, None),
    )
    return jax.shard_map(
        on_device,
        mesh=fine,
        in_specs=placed,
        out_specs=(P(VOX, None, None), P(SEN, VOX, None)),
        check_vma=False,
    )
```
